256 devices in a mesh: space: 64 (over x, z, core), slide: 4 (over y).
Axes of the slice: x: 4, y: 4, z: 8, core: 2. Of those that a mesh axis runs over, the one named last changes fastest.
Arguments:
- image: bfloat16 [4, 96, 1024, 128], P('slide', None, 'space'), may hold values from -6 to 6
- cotangent: bfloat16 [4, 96, 1024, 128], P('slide', None, 'space'), may hold values from -6 to 6
- tissue: int32 [4, 64, 8], P('slide', 'space'), may hold values from 0 to 1, as said below
- dw_kernel: float32 [96, 49], replicated, may hold values from -0.875 to 0.875
- dw_bias: float32 [96], replicated, may hold values from -3 to 3
- ln_gain: float32 [96], replicated, may hold values from 0.5 to 1.5
- ln_bias: float32 [96], replicated, may hold values from -2 to 2
- w_in: bfloat16 [96, 384], replicated, may hold values from -0.625 to 0.625
- b_in: float32 [384], replicated, may hold values from -3 to 3
- w_out: bfloat16 [96, 384], replicated, may hold values from -0.3125 to 0.3125
- b_out: float32 [96], replicated, may hold values from -3 to 3
- layer_scale: float32 [96], replicated, may hold values from 0.4 to 1.2
Outputs:
- out_image: bfloat16 [4, 96, 1024, 128], P('slide', None, 'space')
- grad_image: bfloat16 [4, 96, 1024, 128], P('slide', None, 'space')
- grad_mlp: float32 [2, 96, 384], replicated
- grad_kernel: float32 [96, 49], replicated
- grad_vectors: float32 [5, 96], replicated
- grad_b_in: float32 [384], replicated
The draws below stay inside these ranges and needn't reach their ends.
Inputs may be any that keep to these rules, and one draw needn't show every extreme that they name: In every slide, each of the 8 tiles of one index of space is either tissue or not.
All inputs are finite; a program needn't handle non-finite values.
Results may differ from the reference program's by a relative error of at most 0.007.
Values may be sent and summed in bfloat16 or wider, within the bound.
A program may use at most 64 MiB of HBM per device.

```python
import math
import jax
import jax.numpy as jnp
from jax import lax

C = 96
FF = 384
TP = 16
TROWS = 8
TCOL_DEV = 1
MOST = 8
TCOLS = 64
SLIDES = 4
SLAB_W = 1024
SLAB_H = 128
PIX_ALL = 524288
N_SPACE = 64


def draw_tissue(key, part):
    dev_count = TCOLS // TCOL_DEV
    half_way = dev_count // 2
    tile_count = TCOL_DEV * TROWS
    key_count, key_pair, key_side, key_order = jax.random.split(key, 4)
    low_counts = jax.random.randint(key_count, (SLIDES, half_way), 0, MOST + 1)
    forced = jax.random.randint(key_pair, (SLIDES, 1), 0, half_way)
    extreme = jax.random.randint(key_side, (SLIDES, 1), 0, 2) * MOST
    low_counts = jnp.where(jnp.arange(half_way)[None, :] == forced, extreme, low_counts)
    counts = jnp.concatenate([low_counts, MOST - low_counts], axis=1)
    scores = jax.random.randint(key_order, (SLIDES, dev_count, tile_count), 0, 1048576) * tile_count + jnp.arange(tile_count)[None, None, :]
    tile_ranks = jnp.argsort(jnp.argsort(scores, axis=-1), axis=-1)
    live_tiles = (tile_ranks < counts[:, :, None]).astype(jnp.int32)
    return live_tiles.reshape(SLIDES, dev_count * TCOL_DEV, TROWS)


def level_of(key, dims, cuts, smallest, high):
    loudness, own = 1.0, jax.random.fold_in(key, 6)
    for dim, blocks in cuts:
        steps = jnp.exp(jax.random.uniform(jax.random.fold_in(own, dim), (blocks,), jnp.float32, smallest / len(cuts), high / len(cuts)))
        loudness = loudness * jnp.repeat(steps, dims[dim] // blocks).reshape([-1 if axis == dim else 1 for axis in range(len(dims))])
    return loudness


def normal_values(rng, shape, deviation, limit, shards=(), kind=jnp.bfloat16):
    drawn = deviation * jax.random.normal(rng, shape, jnp.float32)
    if shards:
        drawn = drawn * level_of(rng, shape, shards, -0.22, 0.18)
    return jnp.clip(drawn, -limit, limit).astype(kind)


def setup_inputs(seed: int = 0) -> dict:
    splits = jax.random.split(jax.random.key(seed), 13)
    return {
        "image": normal_values(splits[0], (SLIDES, C, SLAB_W, SLAB_H), 1.0, 6.0, ((0, 4), (2, 64))),
        "cotangent": normal_values(splits[1], (SLIDES, C, SLAB_W, SLAB_H), 1.0, 6.0, ((0, 4), (2, 64))),
        "tissue": draw_tissue(jax.random.fold_in(splits[12], 71), 0),
        "dw_kernel": normal_values(splits[3], (C, 49), 49 ** -0.5, 0.875, (), jnp.float32),
        "dw_bias": normal_values(splits[4], (C,), 0.5, 3.0, (), jnp.float32),
        "ln_gain": jnp.clip(jax.random.uniform(splits[5], (C,), jnp.float32, 0.5, 1.5), 0.5, 1.5),
        "ln_bias": normal_values(splits[6], (C,), 0.3, 2.0, (), jnp.float32),
        "w_in": normal_values(splits[7], (C, FF), C ** -0.5, 0.625),
        "b_in": normal_values(splits[8], (FF,), 0.5, 3.0, (), jnp.float32),
        "w_out": normal_values(splits[9], (C, FF), FF ** -0.5, 0.3125),
        "b_out": normal_values(splits[10], (C,), 0.5, 3.0, (), jnp.float32),
        "layer_scale": jnp.clip(jax.random.uniform(splits[11], (C,), jnp.float32, 0.4, 1.2), 0.4, 1.2),
    }


RADIUS = 3
KERNEL_SIDE = 7
EPSILON = 1e-06
GRAD_COEF = 4.0

def rounded(values):
    return lax.optimization_barrier(values.astype(jnp.bfloat16))

def gelu_value(values):
    return 0.5 * values * (1.0 + jax.scipy.special.erf(values * (1.0 / math.sqrt(2.0))))

def gelu_slope(values):
    return 0.5 * (1.0 + jax.scipy.special.erf(values * (1.0 / math.sqrt(2.0)))) + values * jnp.exp(-0.5 * values * values) * (1.0 / math.sqrt(2.0 * math.pi))

def depthwise(padded, kernel, strip_w, strip_h):
    result = jnp.zeros((padded.shape[0], strip_w, strip_h), jnp.float32)
    for k_row in range(KERNEL_SIDE):
        for k_col in range(KERNEL_SIDE):
            weight = kernel[:, k_row * KERNEL_SIDE + k_col][:, None, None]
            result = result + weight * padded[:, k_row:k_row + strip_w, k_col:k_col + strip_h].astype(jnp.float32)
    return result

def kernel_sums(padded, grad_pre, strip_w, strip_h):
    grad_f = grad_pre.astype(jnp.float32)
    entries = []
    for k_row in range(KERNEL_SIDE):
        for k_col in range(KERNEL_SIDE):
            piece = padded[:, k_row:k_row + strip_w, k_col:k_col + strip_h].astype(jnp.float32)
            entries.append(lax.optimization_barrier(jnp.sum(grad_f * piece, axis=(1, 2))))
    return jnp.stack(entries, axis=1)

def to_tiles(planes):
    channels = planes.shape[0]
    shaped = planes.reshape(channels, TCOL_DEV, TP, TROWS, TP).transpose(1, 3, 0, 2, 4)
    return shaped.reshape(TCOL_DEV * TROWS, channels, TP * TP)

def from_tiles(tiles_in):
    channels = tiles_in.shape[1]
    shaped = tiles_in.reshape(TCOL_DEV, TROWS, channels, TP, TP).transpose(2, 0, 3, 1, 4)
    return shaped.reshape(channels, TCOL_DEV * TP, TROWS * TP)

def mlp_slots(w_in, w_out, b_in, b_out, x_slots, d_slots):
    flt = jnp.float32
    pre_act = jnp.einsum('cf,scp->sfp', w_in.astype(flt), x_slots.astype(flt)) + b_in[None, :, None]
    hidden = rounded(gelu_value(pre_act))
    mlp_out = rounded(jnp.einsum('cf,sfp->scp', w_out.astype(flt), hidden.astype(flt)) + b_out[None, :, None])
    back_hid = jnp.einsum('cf,scp->sfp', w_out.astype(flt), d_slots.astype(flt))
    grad_act = rounded(back_hid * gelu_slope(pre_act))
    grad_ln = rounded(jnp.einsum('cf,sfp->scp', w_in.astype(flt), grad_act.astype(flt)))
    gw_in = jnp.einsum('scp,sfp->cf', x_slots.astype(flt), grad_act.astype(flt))
    gw_out = jnp.einsum('scp,sfp->cf', d_slots.astype(flt), hidden.astype(flt))
    gb_in = lax.optimization_barrier(jnp.sum(grad_act.astype(flt), axis=(0, 2)))
    gb_out = lax.optimization_barrier(jnp.sum(d_slots.astype(flt), axis=(0, 2)))
    return (mlp_out, grad_ln, gw_in, gw_out, gb_in, gb_out)

def reference(image, cotangent, tissue, dw_kernel, dw_bias, ln_gain, ln_bias, w_in, b_in, w_out, b_out, layer_scale):
    flt = jnp.float32
    strip_w = TCOL_DEV * TP
    strip_h = SLAB_H
    gscale = GRAD_COEF / math.sqrt(PIX_ALL)
    flipped = dw_kernel[:, ::-1]

    def per_slide(inputs):
        slide_img, slide_cot, slide_tis = inputs
        pixel_mask = jnp.repeat(jnp.repeat(slide_tis, TP, axis=0), TP, axis=1).astype(jnp.bfloat16)
        masked = slide_img * pixel_mask[None]
        x_padded = jnp.pad(masked, ((0, 0), (RADIUS, RADIUS), (RADIUS, RADIUS)))
        zero_at = jnp.zeros((), jnp.int32)

        def forward_strip(strip_no):
            start = (strip_no * strip_w).astype(jnp.int32)
            padded = lax.dynamic_slice(x_padded, (zero_at, start, zero_at), (C, strip_w + 2 * RADIUS, strip_h + 2 * RADIUS))
            live_tiles = lax.dynamic_slice(slide_tis, ((strip_no * TCOL_DEV).astype(jnp.int32), zero_at), (TCOL_DEV, TROWS))
            cot_strip = lax.dynamic_slice(slide_cot, (zero_at, start, zero_at), (C, strip_w, strip_h))
            pix_strip = lax.dynamic_slice(pixel_mask, (start, zero_at), (strip_w, strip_h))[None].astype(flt)
            masked_strip = padded[:, RADIUS:RADIUS + strip_w, RADIUS:RADIUS + strip_h]
            pre = depthwise(padded, dw_kernel, strip_w, strip_h) + dw_bias[:, None, None]
            centered = pre - lax.optimization_barrier(jnp.mean(pre, axis=0, keepdims=True))
            inv_std = lax.rsqrt(lax.optimization_barrier(jnp.mean(centered * centered, axis=0, keepdims=True)) + EPSILON)
            normed = centered * inv_std
            ln_out = rounded(normed * ln_gain[:, None, None] + ln_bias[:, None, None])
            grad_mix = rounded(cot_strip.astype(flt) * pix_strip * layer_scale[:, None, None])
            flat_live = live_tiles.reshape(-1)
            tile_count = flat_live.shape[0]
            tile_order = jnp.argsort((1 - flat_live) * tile_count + jnp.arange(tile_count, dtype=jnp.int32))
            slot_index = tile_order[:MOST].astype(jnp.int32)
            own_x = to_tiles(ln_out)[slot_index]
            own_d = to_tiles(grad_mix)[slot_index]
            mo_slots, dxh_slots, gw_in, gw_out, gb_in, gb_out = mlp_slots(w_in, w_out, b_in, b_out, own_x, own_d)
            tile_rank = jnp.clip(jnp.cumsum(flat_live) - 1, 0, MOST - 1).astype(jnp.int32)
            keep_tile = flat_live.astype(jnp.bfloat16)[:, None, None]
            mlp_out = from_tiles(mo_slots[tile_rank] * keep_tile)
            grad_ln = from_tiles(dxh_slots[tile_rank] * keep_tile)
            out_strip = (pix_strip * (masked_strip.astype(flt) + layer_scale[:, None, None] * mlp_out.astype(flt))).astype(jnp.bfloat16)
            q_term = grad_ln.astype(flt) * ln_gain[:, None, None]
            grad_pre = rounded(inv_std * (q_term - lax.optimization_barrier(jnp.mean(q_term, axis=0, keepdims=True)) - normed * lax.optimization_barrier(jnp.mean(q_term * normed, axis=0, keepdims=True))))
            grad_k = kernel_sums(padded, grad_pre, strip_w, strip_h)
            vectors = jnp.stack([lax.optimization_barrier(jnp.sum(grad_pre.astype(flt), axis=(1, 2))), lax.optimization_barrier(jnp.sum(grad_ln.astype(flt) * normed, axis=(1, 2))), lax.optimization_barrier(jnp.sum(grad_ln.astype(flt), axis=(1, 2))), gb_out, lax.optimization_barrier(jnp.sum(cot_strip.astype(flt) * pix_strip * mlp_out.astype(flt), axis=(1, 2)))], axis=0)
            return (out_strip, grad_pre, grad_k, vectors, jnp.stack([gw_in, gw_out], axis=0), gb_in)
        strip_ids = jnp.arange(N_SPACE, dtype=jnp.int32)
        out_strips, pre_strips, grad_ks, vector_parts, mlp_parts, bin_parts = lax.map(forward_strip, strip_ids)
        out_full = out_strips.transpose(1, 0, 2, 3).reshape(C, SLAB_W, SLAB_H)
        grad_pre_full = pre_strips.transpose(1, 0, 2, 3).reshape(C, SLAB_W, SLAB_H)
        g_padded = jnp.pad(grad_pre_full, ((0, 0), (RADIUS, RADIUS), (RADIUS, RADIUS)))

        def backward_strip(strip_no):
            start = (strip_no * strip_w).astype(jnp.int32)
            g_strip = lax.dynamic_slice(g_padded, (zero_at, start, zero_at), (C, strip_w + 2 * RADIUS, strip_h + 2 * RADIUS))
            cot_strip = lax.dynamic_slice(slide_cot, (zero_at, start, zero_at), (C, strip_w, strip_h))
            pix_strip = lax.dynamic_slice(pixel_mask, (start, zero_at), (strip_w, strip_h))[None].astype(flt)
            back_conv = depthwise(g_strip, flipped, strip_w, strip_h)
            return (pix_strip * (cot_strip.astype(flt) + back_conv)).astype(jnp.bfloat16)
        grad_strips = lax.map(backward_strip, strip_ids)
        grad_full = grad_strips.transpose(1, 0, 2, 3).reshape(C, SLAB_W, SLAB_H)
        return (out_full, grad_full, lax.optimization_barrier(jnp.sum(grad_ks, axis=0)), lax.optimization_barrier(jnp.sum(vector_parts, axis=0)), lax.optimization_barrier(jnp.sum(mlp_parts, axis=0)), lax.optimization_barrier(jnp.sum(bin_parts, axis=0)))
    out_image, grad_image, grad_ks, vector_parts, mlp_parts, bin_parts = lax.map(per_slide, (image, cotangent, tissue))
    grad_mlp = lax.optimization_barrier(jnp.sum(mlp_parts, axis=0)) * gscale
    grad_kernel = lax.optimization_barrier(jnp.sum(grad_ks, axis=0)) * gscale
    grad_vectors = lax.optimization_barrier(jnp.sum(vector_parts, axis=0)) * gscale
    grad_b_in = lax.optimization_barrier(jnp.sum(bin_parts, axis=0)) * gscale
    return (out_image, grad_image, grad_mlp, grad_kernel, grad_vectors, grad_b_in)
```

```python
import math

import jax
import jax.numpy as jnp
from jax import lax
from jax.sharding import PartitionSpec as P

TP = 16
TROWS = 8
TCOL_DEV = 1
MOST = 8


RADIUS = 3
KERNEL_SIDE = 7
EPSILON = 1e-06
GRAD_COEF = 4.0


def extended(block, sides, width):
    for axis, dim in sides:
        count = lax.axis_size(axis)
        forward = [(i, i + 1) for i in range(count - 1)]
        backward = [(target, source) for source, target in forward]
        low = lax.ppermute(
            lax.slice_in_dim(block, block.shape[dim] - width, None, axis=dim), axis, forward
        )
        high = lax.ppermute(lax.slice_in_dim(block, 0, width, axis=dim), axis, backward)
        block = jnp.concatenate([low, block, high], axis=dim)
    return block


def exchanged(values, axis, stride):
    count = lax.axis_size(axis)
    return lax.ppermute(values, axis, [(i, i ^ stride) for i in range(count)])


def summed_everywhere(parts, axes, lanes=128):
    flat = jnp.concatenate([p.reshape(-1) for p in parts])
    rows = -(-flat.shape[0] // lanes)
    rows += (-rows) % 128
    block = jnp.pad(flat, (0, rows * lanes - flat.shape[0])).reshape(rows, lanes)
    steps = []
    for axis in axes:
        stride = 1
        while stride < lax.axis_size(axis):
            height = block.shape[0]
            if height % 2:
                block = block + exchanged(block, axis, stride)
                steps.append((axis, stride, None))
            else:
                half = height // 2
                upper = (lax.axis_index(axis) // stride) % 2 == 1
                keep = jnp.where(upper, block[half:], block[:half])
                send = jnp.where(upper, block[:half], block[half:])
                block = keep + exchanged(send, axis, stride)
                steps.append((axis, stride, upper))
            stride *= 2
    for axis, stride, upper in reversed(steps):
        if upper is None:
            continue
        got = exchanged(block, axis, stride)
        block = jnp.where(
            upper, jnp.concatenate([got, block]), jnp.concatenate([block, got])
        )
    flat = block.reshape(-1)
    out, start = [], 0
    for p in parts:
        out.append(flat[start : start + p.size].reshape(p.shape))
        start += p.size
    return tuple(out)


def rounded(values):
    return lax.optimization_barrier(values.astype(jnp.bfloat16))


def gelu_value(values):
    return 0.5 * values * (1.0 + jax.scipy.special.erf(values * (1.0 / math.sqrt(2.0))))


def gelu_slope(values):
    return 0.5 * (1.0 + jax.scipy.special.erf(values * (1.0 / math.sqrt(2.0)))) + values * jnp.exp(
        -0.5 * values * values
    ) * (1.0 / math.sqrt(2.0 * math.pi))


def depthwise(padded, kernel, strip_w, strip_h):
    result = jnp.zeros((padded.shape[0], strip_w, strip_h), jnp.float32)
    for k_row in range(KERNEL_SIDE):
        for k_col in range(KERNEL_SIDE):
            weight = kernel[:, k_row * KERNEL_SIDE + k_col][:, None, None]
            result = result + weight * padded[
                :, k_row : k_row + strip_w, k_col : k_col + strip_h
            ].astype(jnp.float32)
    return result


def kernel_sums(padded, grad_pre, strip_w, strip_h):
    grad_f = grad_pre.astype(jnp.float32)
    entries = []
    for k_row in range(KERNEL_SIDE):
        for k_col in range(KERNEL_SIDE):
            piece = padded[:, k_row : k_row + strip_w, k_col : k_col + strip_h].astype(jnp.float32)
            entries.append(jnp.sum(grad_f * piece, axis=(1, 2)))
    return jnp.stack(entries, axis=1)


def to_tiles(planes):
    channels = planes.shape[0]
    shaped = planes.reshape(channels, TCOL_DEV, TP, TROWS, TP).transpose(1, 3, 0, 2, 4)
    return shaped.reshape(TCOL_DEV * TROWS, channels, TP * TP)


def from_tiles(tiles_in):
    channels = tiles_in.shape[1]
    shaped = tiles_in.reshape(TCOL_DEV, TROWS, channels, TP, TP).transpose(2, 0, 3, 1, 4)
    return shaped.reshape(channels, TCOL_DEV * TP, TROWS * TP)


def mlp_slots(w_in, w_out, b_in, b_out, x_slots, d_slots):
    flt = jnp.float32
    pre_act = (
        jnp.einsum("cf,scp->sfp", w_in, x_slots, preferred_element_type=flt) + b_in[None, :, None]
    )
    hidden = rounded(gelu_value(pre_act))
    mlp_out = rounded(
        jnp.einsum("cf,sfp->scp", w_out, hidden, preferred_element_type=flt) + b_out[None, :, None]
    )
    back_hid = jnp.einsum("cf,scp->sfp", w_out, d_slots, preferred_element_type=flt)
    grad_act = rounded(back_hid * gelu_slope(pre_act))
    grad_ln = rounded(jnp.einsum("cf,sfp->scp", w_in, grad_act, preferred_element_type=flt))
    gw_in = jnp.einsum("scp,sfp->cf", x_slots, grad_act, preferred_element_type=flt)
    gw_out = jnp.einsum("scp,sfp->cf", d_slots, hidden, preferred_element_type=flt)
    gb_in = jnp.sum(grad_act.astype(flt), axis=(0, 2))
    gb_out = jnp.sum(d_slots.astype(flt), axis=(0, 2))
    return (mlp_out, grad_ln, gw_in, gw_out, gb_in, gb_out)


def on_device(
    image,
    cotangent,
    tissue,
    dw_kernel,
    dw_bias,
    ln_gain,
    ln_bias,
    w_in,
    b_in,
    w_out,
    b_out,
    layer_scale,
):
    flt = jnp.float32
    strip_w = image.shape[2]
    strip_h = image.shape[3]
    gscale = GRAD_COEF / math.sqrt(
        lax.axis_size("space") * lax.axis_size("slide") * strip_w * strip_h
    )
    live_tiles = tissue[0]
    pixel_mask = jnp.repeat(jnp.repeat(live_tiles, TP, axis=0), TP, axis=1).astype(jnp.bfloat16)
    pix_f = pixel_mask[None].astype(flt)
    masked = image[0] * pixel_mask[None]
    rimmed = extended(masked, (("space", 1),), RADIUS)
    padded = jnp.pad(rimmed, ((0, 0), (0, 0), (RADIUS, RADIUS)))
    pre = depthwise(padded, dw_kernel, strip_w, strip_h) + dw_bias[:, None, None]
    centered = pre - jnp.mean(pre, axis=0, keepdims=True)
    inv_std = lax.rsqrt(jnp.mean(centered * centered, axis=0, keepdims=True) + EPSILON)
    normed = centered * inv_std
    ln_out = rounded(normed * ln_gain[:, None, None] + ln_bias[:, None, None])
    cot_f = cotangent[0].astype(flt)
    grad_mix = rounded(cot_f * pix_f * layer_scale[:, None, None])
    flat_live = live_tiles.reshape(-1)
    tile_count = flat_live.shape[0]
    tile_order = jnp.argsort((1 - flat_live) * tile_count + jnp.arange(tile_count, dtype=jnp.int32))
    own_x = to_tiles(ln_out)[tile_order]
    own_d = to_tiles(grad_mix)[tile_order]
    mo_slots, dxh_slots, gw_in, gw_out, gb_in, gb_out = mlp_slots(
        w_in, w_out, b_in, b_out, own_x, own_d
    )
    tile_rank = jnp.clip(jnp.cumsum(flat_live) - 1, 0, MOST - 1)
    keep_tile = flat_live.astype(jnp.bfloat16)[:, None, None]
    mlp_out = from_tiles(mo_slots[tile_rank] * keep_tile)
    grad_ln = from_tiles(dxh_slots[tile_rank] * keep_tile)
    out_image = (
        pix_f * (masked.astype(flt) + layer_scale[:, None, None] * mlp_out.astype(flt))
    ).astype(jnp.bfloat16)
    q_term = grad_ln.astype(flt) * ln_gain[:, None, None]
    grad_pre = rounded(
        inv_std
        * (
            q_term
            - jnp.mean(q_term, axis=0, keepdims=True)
            - normed * jnp.mean(q_term * normed, axis=0, keepdims=True)
        )
    )
    grad_rim = extended(grad_pre, (("space", 1),), RADIUS)
    grad_padded = jnp.pad(grad_rim, ((0, 0), (0, 0), (RADIUS, RADIUS)))
    back_conv = depthwise(grad_padded, dw_kernel[:, ::-1], strip_w, strip_h)
    grad_image = (pix_f * (cot_f + back_conv)).astype(jnp.bfloat16)
    grad_k = kernel_sums(padded, grad_pre, strip_w, strip_h) * gscale
    vectors = (
        jnp.stack(
            [
                jnp.sum(grad_pre.astype(flt), axis=(1, 2)),
                jnp.sum(grad_ln.astype(flt) * normed, axis=(1, 2)),
                jnp.sum(grad_ln.astype(flt), axis=(1, 2)),
                gb_out,
                jnp.sum(cot_f * pix_f * mlp_out.astype(flt), axis=(1, 2)),
            ],
            axis=0,
        )
        * gscale
    )
    local_mlp = jnp.stack([gw_in, gw_out], axis=0) * gscale
    grad_mlp, grad_kernel, grad_vectors, grad_b_in = summed_everywhere(
        (local_mlp, grad_k, vectors, gb_in * gscale), ("space", "slide")
    )
    return (out_image[None], grad_image[None], grad_mlp, grad_kernel, grad_vectors, grad_b_in)


def solution(mesh):
    placed = (
        P("slide", None, "space", None),
        P("slide", None, "space", None),
        P("slide", "space", None),
        P(),
        P(),
        P(),
        P(),
        P(),
        P(),
        P(),
        P(),
        P(),
    )
    return jax.shard_map(
        on_device,
        mesh=mesh,
        in_specs=placed,
        out_specs=(
            P("slide", None, "space", None),
            P("slide", None, "space", None),
            P(),
            P(),
            P(),
            P(),
        ),
        check_vma=False,
    )
```

```python
import math

import jax
import jax.numpy as jnp
from jax import lax
from jax.sharding import PartitionSpec as P

TP = 16
TROWS = 8
TCOL_DEV = 1
MOST = 8


RADIUS = 3
KERNEL_SIDE = 7
EPSILON = 1e-06
GRAD_COEF = 4.0


def extended(block, sides, width):
    for axis, dim in sides:
        count = lax.axis_size(axis)
        forward = [(i, i + 1) for i in range(count - 1)]
        backward = [(target, source) for source, target in forward]
        low = lax.ppermute(
            lax.slice_in_dim(block, block.shape[dim] - width, None, axis=dim), axis, forward
        )
        high = lax.ppermute(lax.slice_in_dim(block, 0, width, axis=dim), axis, backward)
        block = jnp.concatenate([low, block, high], axis=dim)
    return block


def exchanged(values, axis, stride):
    count = lax.axis_size(axis)
    return lax.ppermute(values, axis, [(i, i ^ stride) for i in range(count)])


def summed_everywhere(parts, axes, lanes=128):
    flat = jnp.concatenate([p.reshape(-1) for p in parts])
    rows = -(-flat.shape[0] // lanes)
    rows += (-rows) % 128
    block = jnp.pad(flat, (0, rows * lanes - flat.shape[0])).reshape(rows, lanes)
    steps = []
    for axis in axes:
        stride = 1
        while stride < lax.axis_size(axis):
            height = block.shape[0]
            if height % 2:
                block = block + exchanged(block, axis, stride)
                steps.append((axis, stride, None))
            else:
                half = height // 2
                upper = (lax.axis_index(axis) // stride) % 2 == 1
                keep = jnp.where(upper, block[half:], block[:half])
                send = jnp.where(upper, block[:half], block[half:])
                block = keep + exchanged(send, axis, stride)
                steps.append((axis, stride, upper))
            stride *= 2
    for axis, stride, upper in reversed(steps):
        if upper is None:
            continue
        got = exchanged(block, axis, stride)
        block = jnp.where(
            upper, jnp.concatenate([got, block]), jnp.concatenate([block, got])
        )
    flat = block.reshape(-1)
    out, start = [], 0
    for p in parts:
        out.append(flat[start : start + p.size].reshape(p.shape))
        start += p.size
    return tuple(out)


def rounded(values):
    return lax.optimization_barrier(values.astype(jnp.bfloat16))


def gelu_value(values):
    return 0.5 * values * (1.0 + jax.scipy.special.erf(values * (1.0 / math.sqrt(2.0))))


def gelu_slope(values):
    return 0.5 * (1.0 + jax.scipy.special.erf(values * (1.0 / math.sqrt(2.0)))) + values * jnp.exp(
        -0.5 * values * values
    ) * (1.0 / math.sqrt(2.0 * math.pi))


def depthwise(padded, kernel, strip_w, strip_h):
    result = jnp.zeros((padded.shape[0], strip_w, strip_h), jnp.float32)
    for k_row in range(KERNEL_SIDE):
        for k_col in range(KERNEL_SIDE):
            weight = kernel[:, k_row * KERNEL_SIDE + k_col][:, None, None]
            result = result + weight * padded[
                :, k_row : k_row + strip_w, k_col : k_col + strip_h
            ].astype(jnp.float32)
    return result


def kernel_sums(padded, grad_pre, strip_w, strip_h):
    grad_f = grad_pre.astype(jnp.float32)
    entries = []
    for k_row in range(KERNEL_SIDE):
        for k_col in range(KERNEL_SIDE):
            piece = padded[:, k_row : k_row + strip_w, k_col : k_col + strip_h].astype(jnp.float32)
            entries.append(jnp.sum(grad_f * piece, axis=(1, 2)))
    return jnp.stack(entries, axis=1)


def to_tiles(planes):
    channels = planes.shape[0]
    shaped = planes.reshape(channels, TCOL_DEV, TP, TROWS, TP).transpose(1, 3, 0, 2, 4)
    return shaped.reshape(TCOL_DEV * TROWS, channels, TP * TP)


def from_tiles(tiles_in):
    channels = tiles_in.shape[1]
    shaped = tiles_in.reshape(TCOL_DEV, TROWS, channels, TP, TP).transpose(2, 0, 3, 1, 4)
    return shaped.reshape(channels, TCOL_DEV * TP, TROWS * TP)


def mlp_pixels(w_in, w_out, b_in, b_out, x_pix, d_pix):
    flt = jnp.float32
    pre_act = jnp.einsum("cf,cp->fp", w_in, x_pix, preferred_element_type=flt) + b_in[:, None]
    hidden = rounded(gelu_value(pre_act))
    mlp_out = rounded(
        jnp.einsum("cf,fp->cp", w_out, hidden, preferred_element_type=flt) + b_out[:, None]
    )
    back_hid = jnp.einsum("cf,cp->fp", w_out, d_pix, preferred_element_type=flt)
    grad_act = rounded(back_hid * gelu_slope(pre_act))
    grad_ln = rounded(jnp.einsum("cf,fp->cp", w_in, grad_act, preferred_element_type=flt))
    gw_in = jnp.einsum("cp,fp->cf", x_pix, grad_act, preferred_element_type=flt)
    gw_out = jnp.einsum("cp,fp->cf", d_pix, hidden, preferred_element_type=flt)
    gb_in = jnp.sum(grad_act.astype(flt), axis=1)
    gb_out = jnp.sum(d_pix.astype(flt), axis=1)
    return (mlp_out, grad_ln, gw_in, gw_out, gb_in, gb_out)


def on_device(
    image,
    cotangent,
    tissue,
    dw_kernel,
    dw_bias,
    ln_gain,
    ln_bias,
    w_in,
    b_in,
    w_out,
    b_out,
    layer_scale,
):
    flt = jnp.float32
    strip_w = image.shape[2]
    strip_h = image.shape[3]
    gscale = GRAD_COEF / math.sqrt(
        lax.axis_size("space") * lax.axis_size("slide") * strip_w * strip_h
    )
    live_tiles = tissue[0]
    pixel_mask = jnp.repeat(jnp.repeat(live_tiles, TP, axis=0), TP, axis=1).astype(jnp.bfloat16)
    pix_f = pixel_mask[None].astype(flt)
    masked = image[0] * pixel_mask[None]
    rimmed = extended(masked, (("space", 1),), RADIUS)
    padded = jnp.pad(rimmed, ((0, 0), (0, 0), (RADIUS, RADIUS)))
    pre = depthwise(padded, dw_kernel, strip_w, strip_h) + dw_bias[:, None, None]
    centered = pre - jnp.mean(pre, axis=0, keepdims=True)
    inv_std = lax.rsqrt(jnp.mean(centered * centered, axis=0, keepdims=True) + EPSILON)
    normed = centered * inv_std
    ln_out = rounded(normed * ln_gain[:, None, None] + ln_bias[:, None, None])
    cot_f = cotangent[0].astype(flt)
    grad_mix = rounded(cot_f * pix_f * layer_scale[:, None, None])
    channels, pixels = ln_out.shape[0], strip_w * strip_h
    mo_flat, dxh_flat, gw_in, gw_out, gb_in, gb_out = mlp_pixels(
        w_in, w_out, b_in, b_out, ln_out.reshape(channels, pixels), grad_mix.reshape(channels, pixels)
    )
    mlp_out = mo_flat.reshape(ln_out.shape) * pixel_mask[None]
    grad_ln = dxh_flat.reshape(ln_out.shape) * pixel_mask[None]
    out_image = (
        pix_f * (masked.astype(flt) + layer_scale[:, None, None] * mlp_out.astype(flt))
    ).astype(jnp.bfloat16)
    q_term = grad_ln.astype(flt) * ln_gain[:, None, None]
    grad_pre = rounded(
        inv_std
        * (
            q_term
            - jnp.mean(q_term, axis=0, keepdims=True)
            - normed * jnp.mean(q_term * normed, axis=0, keepdims=True)
        )
    )
    grad_rim = extended(grad_pre, (("space", 1),), RADIUS)
    grad_padded = jnp.pad(grad_rim, ((0, 0), (0, 0), (RADIUS, RADIUS)))
    back_conv = depthwise(grad_padded, dw_kernel[:, ::-1], strip_w, strip_h)
    grad_image = (pix_f * (cot_f + back_conv)).astype(jnp.bfloat16)
    grad_k = kernel_sums(padded, grad_pre, strip_w, strip_h) * gscale
    vectors = (
        jnp.stack(
            [
                jnp.sum(grad_pre.astype(flt), axis=(1, 2)),
                jnp.sum(grad_ln.astype(flt) * normed, axis=(1, 2)),
                jnp.sum(grad_ln.astype(flt), axis=(1, 2)),
                gb_out,
                jnp.sum(cot_f * pix_f * mlp_out.astype(flt), axis=(1, 2)),
            ],
            axis=0,
        )
        * gscale
    )
    local_mlp = jnp.stack([gw_in, gw_out], axis=0) * gscale
    grad_mlp, grad_kernel, grad_vectors, grad_b_in = summed_everywhere(
        (local_mlp, grad_k, vectors, gb_in * gscale), ("space", "slide")
    )
    return (out_image[None], grad_image[None], grad_mlp, grad_kernel, grad_vectors, grad_b_in)


def solution(mesh):
    placed = (
        P("slide", None, "space", None),
        P("slide", None, "space", None),
        P("slide", "space", None),
        P(),
        P(),
        P(),
        P(),
        P(),
        P(),
        P(),
        P(),
        P(),
    )
    return jax.shard_map(
        on_device,
        mesh=mesh,
        in_specs=placed,
        out_specs=(
            P("slide", None, "space", None),
            P("slide", None, "space", None),
            P(),
            P(),
            P(),
            P(),
        ),
        check_vma=False,
    )
```

```python
import math

import jax
import jax.numpy as jnp
from jax import lax
from jax.sharding import PartitionSpec as P

TP = 16
TROWS = 8
TCOL_DEV = 1
MOST = 8


RADIUS = 3
KERNEL_SIDE = 7
EPSILON = 1e-06
GRAD_COEF = 4.0


def extended(block, sides, width):
    for axis, dim in sides:
        count = lax.axis_size(axis)
        forward = [(i, i + 1) for i in range(count - 1)]
        backward = [(target, source) for source, target in forward]
        low = lax.ppermute(
            lax.slice_in_dim(block, block.shape[dim] - width, None, axis=dim), axis, forward
        )
        high = lax.ppermute(lax.slice_in_dim(block, 0, width, axis=dim), axis, backward)
        block = jnp.concatenate([low, block, high], axis=dim)
    return block


def shifted(values, axis, stride, radix, shift):
    pairs = []
    for i in range(lax.axis_size(axis)):
        digit = (i // stride) % radix
        pairs.append((i, i + ((digit + shift) % radix - digit) * stride))
    return lax.ppermute(values, axis, pairs)


def digit_groups(axes):
    groups = []
    for axis in axes:
        stride, size = 1, lax.axis_size(axis)
        while stride < size:
            radix = 4 if size % (stride * 4) == 0 else 2
            groups.append((axis, stride, radix))
            stride *= radix
    return groups


def summed_everywhere(parts, axes, lanes=128):
    flat = jnp.concatenate([p.reshape(-1) for p in parts])
    rows = -(-flat.shape[0] // lanes)
    rows += (-rows) % 128
    block = jnp.pad(flat, (0, rows * lanes - flat.shape[0])).reshape(rows, lanes)
    steps = []
    for axis, stride, radix in digit_groups(axes):
        digit = (lax.axis_index(axis) // stride) % radix
        height, rest = divmod(block.shape[0], radix)
        if rest:
            stack = jnp.zeros((radix,) + block.shape, block.dtype)
            stack = lax.dynamic_update_index_in_dim(stack, block, digit, 0)
            for shift in range(1, radix):
                got = shifted(block, axis, stride, radix, shift)
                stack = lax.dynamic_update_index_in_dim(stack, got, (digit - shift) % radix, 0)
            block = stack[0]
            for k in range(1, radix):
                block = block + stack[k]
            continue
        keep = lax.dynamic_slice_in_dim(block, digit * height, height)
        for shift in range(1, radix):
            send = lax.dynamic_slice_in_dim(block, ((digit + shift) % radix) * height, height)
            keep = keep + shifted(send, axis, stride, radix, shift)
        block = keep
        steps.append((axis, stride, radix, digit))
    for axis, stride, radix, digit in reversed(steps):
        height = block.shape[0]
        whole = jnp.zeros((height * radix,) + block.shape[1:], block.dtype)
        whole = lax.dynamic_update_slice_in_dim(whole, block, digit * height, 0)
        for shift in range(1, radix):
            got = shifted(block, axis, stride, radix, shift)
            whole = lax.dynamic_update_slice_in_dim(
                whole, got, ((digit - shift) % radix) * height, 0
            )
        block = whole
    flat = block.reshape(-1)
    out, start = [], 0
    for p in parts:
        out.append(flat[start : start + p.size].reshape(p.shape))
        start += p.size
    return tuple(out)

def rounded(values):
    return lax.optimization_barrier(values.astype(jnp.bfloat16))


def gelu_value(values):
    return 0.5 * values * (1.0 + jax.scipy.special.erf(values * (1.0 / math.sqrt(2.0))))


def gelu_slope(values):
    return 0.5 * (1.0 + jax.scipy.special.erf(values * (1.0 / math.sqrt(2.0)))) + values * jnp.exp(
        -0.5 * values * values
    ) * (1.0 / math.sqrt(2.0 * math.pi))


def depthwise(padded, kernel, strip_w, strip_h):
    result = jnp.zeros((padded.shape[0], strip_w, strip_h), jnp.float32)
    for k_row in range(KERNEL_SIDE):
        for k_col in range(KERNEL_SIDE):
            weight = kernel[:, k_row * KERNEL_SIDE + k_col][:, None, None]
            result = result + weight * padded[
                :, k_row : k_row + strip_w, k_col : k_col + strip_h
            ].astype(jnp.float32)
    return result


def kernel_sums(padded, grad_pre, strip_w, strip_h):
    grad_f = grad_pre.astype(jnp.float32)
    entries = []
    for k_row in range(KERNEL_SIDE):
        for k_col in range(KERNEL_SIDE):
            piece = padded[:, k_row : k_row + strip_w, k_col : k_col + strip_h].astype(jnp.float32)
            entries.append(jnp.sum(grad_f * piece, axis=(1, 2)))
    return jnp.stack(entries, axis=1)


def to_tiles(planes):
    channels = planes.shape[0]
    shaped = planes.reshape(channels, TCOL_DEV, TP, TROWS, TP).transpose(1, 3, 0, 2, 4)
    return shaped.reshape(TCOL_DEV * TROWS, channels, TP * TP)


def from_tiles(tiles_in):
    channels = tiles_in.shape[1]
    shaped = tiles_in.reshape(TCOL_DEV, TROWS, channels, TP, TP).transpose(2, 0, 3, 1, 4)
    return shaped.reshape(channels, TCOL_DEV * TP, TROWS * TP)


def mlp_pixels(w_in, w_out, b_in, b_out, x_pix, d_pix):
    flt = jnp.float32
    pre_act = jnp.einsum("cf,cp->fp", w_in, x_pix, preferred_element_type=flt) + b_in[:, None]
    hidden = rounded(gelu_value(pre_act))
    mlp_out = rounded(
        jnp.einsum("cf,fp->cp", w_out, hidden, preferred_element_type=flt) + b_out[:, None]
    )
    back_hid = jnp.einsum("cf,cp->fp", w_out, d_pix, preferred_element_type=flt)
    grad_act = rounded(back_hid * gelu_slope(pre_act))
    grad_ln = rounded(jnp.einsum("cf,fp->cp", w_in, grad_act, preferred_element_type=flt))
    gw_in = jnp.einsum("cp,fp->cf", x_pix, grad_act, preferred_element_type=flt)
    gw_out = jnp.einsum("cp,fp->cf", d_pix, hidden, preferred_element_type=flt)
    gb_in = jnp.sum(grad_act.astype(flt), axis=1)
    gb_out = jnp.sum(d_pix.astype(flt), axis=1)
    return (mlp_out, grad_ln, gw_in, gw_out, gb_in, gb_out)


def on_device(
    image,
    cotangent,
    tissue,
    dw_kernel,
    dw_bias,
    ln_gain,
    ln_bias,
    w_in,
    b_in,
    w_out,
    b_out,
    layer_scale,
):
    flt = jnp.float32
    strip_w = image.shape[2]
    strip_h = image.shape[3]
    gscale = GRAD_COEF / math.sqrt(
        lax.axis_size("space") * lax.axis_size("slide") * strip_w * strip_h
    )
    live_tiles = tissue[0]
    pixel_mask = jnp.repeat(jnp.repeat(live_tiles, TP, axis=0), TP, axis=1).astype(jnp.bfloat16)
    pix_f = pixel_mask[None].astype(flt)
    masked = image[0] * pixel_mask[None]
    rimmed = extended(masked, (("space", 1),), RADIUS)
    padded = jnp.pad(rimmed, ((0, 0), (0, 0), (RADIUS, RADIUS)))
    pre = depthwise(padded, dw_kernel, strip_w, strip_h) + dw_bias[:, None, None]
    centered = pre - jnp.mean(pre, axis=0, keepdims=True)
    inv_std = lax.rsqrt(jnp.mean(centered * centered, axis=0, keepdims=True) + EPSILON)
    normed = centered * inv_std
    ln_out = rounded(normed * ln_gain[:, None, None] + ln_bias[:, None, None])
    cot_f = cotangent[0].astype(flt)
    grad_mix = rounded(cot_f * pix_f * layer_scale[:, None, None])
    channels, pixels = ln_out.shape[0], strip_w * strip_h
    mo_flat, dxh_flat, gw_in, gw_out, gb_in, gb_out = mlp_pixels(
        w_in, w_out, b_in, b_out, ln_out.reshape(channels, pixels), grad_mix.reshape(channels, pixels)
    )
    mlp_out = mo_flat.reshape(ln_out.shape) * pixel_mask[None]
    grad_ln = dxh_flat.reshape(ln_out.shape) * pixel_mask[None]
    out_image = (
        pix_f * (masked.astype(flt) + layer_scale[:, None, None] * mlp_out.astype(flt))
    ).astype(jnp.bfloat16)
    q_term = grad_ln.astype(flt) * ln_gain[:, None, None]
    grad_pre = rounded(
        inv_std
        * (
            q_term
            - jnp.mean(q_term, axis=0, keepdims=True)
            - normed * jnp.mean(q_term * normed, axis=0, keepdims=True)
        )
    )
    grad_rim = extended(grad_pre, (("space", 1),), RADIUS)
    grad_padded = jnp.pad(grad_rim, ((0, 0), (0, 0), (RADIUS, RADIUS)))
    back_conv = depthwise(grad_padded, dw_kernel[:, ::-1], strip_w, strip_h)
    grad_image = (pix_f * (cot_f + back_conv)).astype(jnp.bfloat16)
    grad_k = kernel_sums(padded, grad_pre, strip_w, strip_h) * gscale
    vectors = (
        jnp.stack(
            [
                jnp.sum(grad_pre.astype(flt), axis=(1, 2)),
                jnp.sum(grad_ln.astype(flt) * normed, axis=(1, 2)),
                jnp.sum(grad_ln.astype(flt), axis=(1, 2)),
                gb_out,
                jnp.sum(cot_f * pix_f * mlp_out.astype(flt), axis=(1, 2)),
            ],
            axis=0,
        )
        * gscale
    )
    local_mlp = jnp.stack([gw_in, gw_out], axis=0) * gscale
    grad_mlp, grad_kernel, grad_vectors, grad_b_in = summed_everywhere(
        (local_mlp, grad_k, vectors, gb_in * gscale), ("space", "slide")
    )
    return (out_image[None], grad_image[None], grad_mlp, grad_kernel, grad_vectors, grad_b_in)


def solution(mesh):
    placed = (
        P("slide", None, "space", None),
        P("slide", None, "space", None),
        P("slide", "space", None),
        P(),
        P(),
        P(),
        P(),
        P(),
        P(),
        P(),
        P(),
        P(),
    )
    return jax.shard_map(
        on_device,
        mesh=mesh,
        in_specs=placed,
        out_specs=(
            P("slide", None, "space", None),
            P("slide", None, "space", None),
            P(),
            P(),
            P(),
            P(),
        ),
        check_vma=False,
    )
```

```python
import math

import jax
import jax.numpy as jnp
from jax import lax
from jax.sharding import PartitionSpec as P

TP = 16
TROWS = 8
TCOL_DEV = 1
MOST = 8


RADIUS = 3
KERNEL_SIDE = 7
EPSILON = 1e-06
GRAD_COEF = 4.0


def extended(block, sides, width):
    for axis, dim in sides:
        count = lax.axis_size(axis)
        forward = [(i, i + 1) for i in range(count - 1)]
        backward = [(target, source) for source, target in forward]
        low = lax.ppermute(
            lax.slice_in_dim(block, block.shape[dim] - width, None, axis=dim), axis, forward
        )
        high = lax.ppermute(lax.slice_in_dim(block, 0, width, axis=dim), axis, backward)
        block = jnp.concatenate([low, block, high], axis=dim)
    return block


def shifted(values, axis, stride, radix, shift):
    pairs = []
    for i in range(lax.axis_size(axis)):
        digit = (i // stride) % radix
        pairs.append((i, i + ((digit + shift) % radix - digit) * stride))
    return lax.ppermute(values, axis, pairs)


def digit_groups(axes):
    groups = []
    for axis in axes:
        stride, size = 1, lax.axis_size(axis)
        while stride < size:
            radix = 4 if size % (stride * 4) == 0 else 2
            groups.append((axis, stride, radix))
            stride *= radix
    return groups


def summed_everywhere(parts, axes, lanes=128):
    flat = jnp.concatenate([p.reshape(-1) for p in parts])
    rows = -(-flat.shape[0] // lanes)
    rows += (-rows) % 128
    block = jnp.pad(flat, (0, rows * lanes - flat.shape[0])).reshape(rows, lanes)
    steps = []
    for axis, stride, radix in digit_groups(axes):
        digit = (lax.axis_index(axis) // stride) % radix
        height, rest = divmod(block.shape[0], radix)
        if rest:
            stack = jnp.zeros((radix,) + block.shape, block.dtype)
            stack = lax.dynamic_update_index_in_dim(stack, block, digit, 0)
            for shift in range(1, radix):
                got = shifted(block, axis, stride, radix, shift)
                stack = lax.dynamic_update_index_in_dim(stack, got, (digit - shift) % radix, 0)
            block = stack[0]
            for k in range(1, radix):
                block = block + stack[k]
            continue
        keep = lax.dynamic_slice_in_dim(block, digit * height, height)
        for shift in range(1, radix):
            send = lax.dynamic_slice_in_dim(block, ((digit + shift) % radix) * height, height)
            keep = keep + shifted(send, axis, stride, radix, shift)
        block = keep
        steps.append((axis, stride, radix, digit))
    for axis, stride, radix, digit in reversed(steps):
        height = block.shape[0]
        whole = jnp.zeros((height * radix,) + block.shape[1:], block.dtype)
        whole = lax.dynamic_update_slice_in_dim(whole, block, digit * height, 0)
        for shift in range(1, radix):
            got = shifted(block, axis, stride, radix, shift)
            whole = lax.dynamic_update_slice_in_dim(
                whole, got, ((digit - shift) % radix) * height, 0
            )
        block = whole
    flat = block.reshape(-1)
    out, start = [], 0
    for p in parts:
        out.append(flat[start : start + p.size].reshape(p.shape))
        start += p.size
    return tuple(out)

def rounded(values):
    return lax.optimization_barrier(values.astype(jnp.bfloat16))


def gelu_value(values):
    return 0.5 * values * (1.0 + jax.scipy.special.erf(values * (1.0 / math.sqrt(2.0))))


def gelu_slope(values):
    return 0.5 * (1.0 + jax.scipy.special.erf(values * (1.0 / math.sqrt(2.0)))) + values * jnp.exp(
        -0.5 * values * values
    ) * (1.0 / math.sqrt(2.0 * math.pi))


def depthwise(padded, kernel, strip_w, strip_h):
    result = jnp.zeros((padded.shape[0], strip_w, strip_h), jnp.float32)
    for k_row in range(KERNEL_SIDE):
        for k_col in range(KERNEL_SIDE):
            weight = kernel[:, k_row * KERNEL_SIDE + k_col][:, None, None]
            result = result + weight * padded[
                :, k_row : k_row + strip_w, k_col : k_col + strip_h
            ].astype(jnp.float32)
    return result


def kernel_sums(padded, grad_pre, strip_w, strip_h):
    channels = padded.shape[0]
    sums = lax.conv_general_dilated(
        padded[None],
        grad_pre[:, None],
        (1, 1),
        "VALID",
        dimension_numbers=("NCHW", "OIHW", "NCHW"),
        feature_group_count=channels,
        preferred_element_type=jnp.float32,
    )
    return sums[0].reshape(channels, KERNEL_SIDE * KERNEL_SIDE)


def to_tiles(planes):
    channels = planes.shape[0]
    shaped = planes.reshape(channels, TCOL_DEV, TP, TROWS, TP).transpose(1, 3, 0, 2, 4)
    return shaped.reshape(TCOL_DEV * TROWS, channels, TP * TP)


def from_tiles(tiles_in):
    channels = tiles_in.shape[1]
    shaped = tiles_in.reshape(TCOL_DEV, TROWS, channels, TP, TP).transpose(2, 0, 3, 1, 4)
    return shaped.reshape(channels, TCOL_DEV * TP, TROWS * TP)


def mlp_pixels(w_in, w_out, b_in, b_out, x_pix, d_pix):
    flt = jnp.float32
    pre_act = jnp.einsum("cf,cp->fp", w_in, x_pix, preferred_element_type=flt) + b_in[:, None]
    hidden = rounded(gelu_value(pre_act))
    mlp_out = rounded(
        jnp.einsum("cf,fp->cp", w_out, hidden, preferred_element_type=flt) + b_out[:, None]
    )
    back_hid = jnp.einsum("cf,cp->fp", w_out, d_pix, preferred_element_type=flt)
    grad_act = rounded(back_hid * gelu_slope(pre_act))
    grad_ln = rounded(jnp.einsum("cf,fp->cp", w_in, grad_act, preferred_element_type=flt))
    gw_in = jnp.einsum("cp,fp->cf", x_pix, grad_act, preferred_element_type=flt)
    gw_out = jnp.einsum("cp,fp->cf", d_pix, hidden, preferred_element_type=flt)
    gb_in = jnp.sum(grad_act.astype(flt), axis=1)
    gb_out = jnp.sum(d_pix.astype(flt), axis=1)
    return (mlp_out, grad_ln, gw_in, gw_out, gb_in, gb_out)


def on_device(
    image,
    cotangent,
    tissue,
    dw_kernel,
    dw_bias,
    ln_gain,
    ln_bias,
    w_in,
    b_in,
    w_out,
    b_out,
    layer_scale,
):
    flt = jnp.float32
    strip_w = image.shape[2]
    strip_h = image.shape[3]
    gscale = GRAD_COEF / math.sqrt(
        lax.axis_size("space") * lax.axis_size("slide") * strip_w * strip_h
    )
    live_tiles = tissue[0]
    pixel_mask = jnp.repeat(jnp.repeat(live_tiles, TP, axis=0), TP, axis=1).astype(jnp.bfloat16)
    pix_f = pixel_mask[None].astype(flt)
    masked = image[0] * pixel_mask[None]
    rimmed = extended(masked, (("space", 1),), RADIUS)
    padded = jnp.pad(rimmed, ((0, 0), (0, 0), (RADIUS, RADIUS)))
    pre = depthwise(padded, dw_kernel, strip_w, strip_h) + dw_bias[:, None, None]
    centered = pre - jnp.mean(pre, axis=0, keepdims=True)
    inv_std = lax.rsqrt(jnp.mean(centered * centered, axis=0, keepdims=True) + EPSILON)
    normed = centered * inv_std
    ln_out = rounded(normed * ln_gain[:, None, None] + ln_bias[:, None, None])
    cot_f = cotangent[0].astype(flt)
    grad_mix = rounded(cot_f * pix_f * layer_scale[:, None, None])
    channels, pixels = ln_out.shape[0], strip_w * strip_h
    mo_flat, dxh_flat, gw_in, gw_out, gb_in, gb_out = mlp_pixels(
        w_in, w_out, b_in, b_out, ln_out.reshape(channels, pixels), grad_mix.reshape(channels, pixels)
    )
    mlp_out = mo_flat.reshape(ln_out.shape) * pixel_mask[None]
    grad_ln = dxh_flat.reshape(ln_out.shape) * pixel_mask[None]
    out_image = (
        pix_f * (masked.astype(flt) + layer_scale[:, None, None] * mlp_out.astype(flt))
    ).astype(jnp.bfloat16)
    q_term = grad_ln.astype(flt) * ln_gain[:, None, None]
    grad_pre = rounded(
        inv_std
        * (
            q_term
            - jnp.mean(q_term, axis=0, keepdims=True)
            - normed * jnp.mean(q_term * normed, axis=0, keepdims=True)
        )
    )
    grad_rim = extended(grad_pre, (("space", 1),), RADIUS)
    grad_padded = jnp.pad(grad_rim, ((0, 0), (0, 0), (RADIUS, RADIUS)))
    back_conv = depthwise(grad_padded, dw_kernel[:, ::-1], strip_w, strip_h)
    grad_image = (pix_f * (cot_f + back_conv)).astype(jnp.bfloat16)
    grad_k = kernel_sums(padded, grad_pre, strip_w, strip_h) * gscale
    vectors = (
        jnp.stack(
            [
                jnp.sum(grad_pre.astype(flt), axis=(1, 2)),
                jnp.sum(grad_ln.astype(flt) * normed, axis=(1, 2)),
                jnp.sum(grad_ln.astype(flt), axis=(1, 2)),
                gb_out,
                jnp.sum(cot_f * pix_f * mlp_out.astype(flt), axis=(1, 2)),
            ],
            axis=0,
        )
        * gscale
    )
    local_mlp = jnp.stack([gw_in, gw_out], axis=0) * gscale
    grad_mlp, grad_kernel, grad_vectors, grad_b_in = summed_everywhere(
        (local_mlp, grad_k, vectors, gb_in * gscale), ("space", "slide")
    )
    return (out_image[None], grad_image[None], grad_mlp, grad_kernel, grad_vectors, grad_b_in)


def solution(mesh):
    placed = (
        P("slide", None, "space", None),
        P("slide", None, "space", None),
        P("slide", "space", None),
        P(),
        P(),
        P(),
        P(),
        P(),
        P(),
        P(),
        P(),
        P(),
    )
    return jax.shard_map(
        on_device,
        mesh=mesh,
        in_specs=placed,
        out_specs=(
            P("slide", None, "space", None),
            P("slide", None, "space", None),
            P(),
            P(),
            P(),
            P(),
        ),
        check_vma=False,
    )
```

```python
import math

import jax
import jax.numpy as jnp
from jax import lax
from jax.sharding import PartitionSpec as P

TP = 16
TROWS = 8
TCOL_DEV = 1
MOST = 8


RADIUS = 3
KERNEL_SIDE = 7
EPSILON = 1e-06
GRAD_COEF = 4.0


def extended(block, sides, width):
    for axis, dim in sides:
        count = lax.axis_size(axis)
        forward = [(i, i + 1) for i in range(count - 1)]
        backward = [(target, source) for source, target in forward]
        low = lax.ppermute(
            lax.slice_in_dim(block, block.shape[dim] - width, None, axis=dim), axis, forward
        )
        high = lax.ppermute(lax.slice_in_dim(block, 0, width, axis=dim), axis, backward)
        block = jnp.concatenate([low, block, high], axis=dim)
    return block


def shifted(values, axis, stride, radix, shift):
    pairs = []
    for i in range(lax.axis_size(axis)):
        digit = (i // stride) % radix
        pairs.append((i, i + ((digit + shift) % radix - digit) * stride))
    return lax.ppermute(values, axis, pairs)


def digit_groups(axes):
    groups = []
    for axis in axes:
        stride, size = 1, lax.axis_size(axis)
        while stride < size:
            radix = 4 if size % (stride * 4) == 0 else 2
            groups.append((axis, stride, radix))
            stride *= radix
    return groups


def summed_everywhere(parts, axes, lanes=128):
    flat = jnp.concatenate([p.reshape(-1) for p in parts])
    rows = -(-flat.shape[0] // lanes)
    rows += (-rows) % 128
    block = jnp.pad(flat, (0, rows * lanes - flat.shape[0])).reshape(rows, lanes)
    steps = []
    for axis, stride, radix in digit_groups(axes):
        digit = (lax.axis_index(axis) // stride) % radix
        height, rest = divmod(block.shape[0], radix)
        if rest:
            stack = jnp.zeros((radix,) + block.shape, block.dtype)
            stack = lax.dynamic_update_index_in_dim(stack, block, digit, 0)
            for shift in range(1, radix):
                got = shifted(block, axis, stride, radix, shift)
                stack = lax.dynamic_update_index_in_dim(stack, got, (digit - shift) % radix, 0)
            block = stack[0]
            for k in range(1, radix):
                block = block + stack[k]
            continue
        keep = lax.dynamic_slice_in_dim(block, digit * height, height)
        for shift in range(1, radix):
            send = lax.dynamic_slice_in_dim(block, ((digit + shift) % radix) * height, height)
            keep = keep + shifted(send, axis, stride, radix, shift)
        block = keep
        steps.append((axis, stride, radix, digit))
    for axis, stride, radix, digit in reversed(steps):
        height = block.shape[0]
        whole = jnp.zeros((height * radix,) + block.shape[1:], block.dtype)
        whole = lax.dynamic_update_slice_in_dim(whole, block, digit * height, 0)
        for shift in range(1, radix):
            got = shifted(block, axis, stride, radix, shift)
            whole = lax.dynamic_update_slice_in_dim(
                whole, got, ((digit - shift) % radix) * height, 0
            )
        block = whole
    flat = block.reshape(-1)
    out, start = [], 0
    for p in parts:
        out.append(flat[start : start + p.size].reshape(p.shape))
        start += p.size
    return tuple(out)

def rounded(values):
    return values.astype(jnp.bfloat16)


def gelu_value(values):
    return 0.5 * values * (1.0 + jax.scipy.special.erf(values * (1.0 / math.sqrt(2.0))))


def gelu_slope(values):
    return 0.5 * (1.0 + jax.scipy.special.erf(values * (1.0 / math.sqrt(2.0)))) + values * jnp.exp(
        -0.5 * values * values
    ) * (1.0 / math.sqrt(2.0 * math.pi))


def depthwise(padded, kernel, strip_w, strip_h):
    result = jnp.zeros((padded.shape[0], strip_w, strip_h), jnp.float32)
    for k_row in range(KERNEL_SIDE):
        for k_col in range(KERNEL_SIDE):
            weight = kernel[:, k_row * KERNEL_SIDE + k_col][:, None, None]
            result = result + weight * padded[
                :, k_row : k_row + strip_w, k_col : k_col + strip_h
            ].astype(jnp.float32)
    return result


def kernel_sums(padded, grad_pre, strip_w, strip_h):
    grad_f = grad_pre.astype(jnp.float32)
    entries = []
    for k_row in range(KERNEL_SIDE):
        for k_col in range(KERNEL_SIDE):
            piece = padded[:, k_row : k_row + strip_w, k_col : k_col + strip_h].astype(jnp.float32)
            entries.append(jnp.sum(grad_f * piece, axis=(1, 2)))
    return jnp.stack(entries, axis=1)


def to_tiles(planes):
    channels = planes.shape[0]
    shaped = planes.reshape(channels, TCOL_DEV, TP, TROWS, TP).transpose(1, 3, 0, 2, 4)
    return shaped.reshape(TCOL_DEV * TROWS, channels, TP * TP)


def from_tiles(tiles_in):
    channels = tiles_in.shape[1]
    shaped = tiles_in.reshape(TCOL_DEV, TROWS, channels, TP, TP).transpose(2, 0, 3, 1, 4)
    return shaped.reshape(channels, TCOL_DEV * TP, TROWS * TP)


def mlp_pixels(w_in, w_out, b_in, b_out, x_pix, d_pix):
    flt = jnp.float32
    pre_act = jnp.einsum("cf,cp->fp", w_in, x_pix, preferred_element_type=flt) + b_in[:, None]
    hidden = rounded(gelu_value(pre_act))
    mlp_out = rounded(
        jnp.einsum("cf,fp->cp", w_out, hidden, preferred_element_type=flt) + b_out[:, None]
    )
    back_hid = jnp.einsum("cf,cp->fp", w_out, d_pix, preferred_element_type=flt)
    grad_act = rounded(back_hid * gelu_slope(pre_act))
    grad_ln = rounded(jnp.einsum("cf,fp->cp", w_in, grad_act, preferred_element_type=flt))
    gw_in = jnp.einsum("cp,fp->cf", x_pix, grad_act, preferred_element_type=flt)
    gw_out = jnp.einsum("cp,fp->cf", d_pix, hidden, preferred_element_type=flt)
    gb_in = jnp.sum(grad_act.astype(flt), axis=1)
    gb_out = jnp.sum(d_pix.astype(flt), axis=1)
    return (mlp_out, grad_ln, gw_in, gw_out, gb_in, gb_out)


def on_device(
    image,
    cotangent,
    tissue,
    dw_kernel,
    dw_bias,
    ln_gain,
    ln_bias,
    w_in,
    b_in,
    w_out,
    b_out,
    layer_scale,
):
    flt = jnp.float32
    strip_w = image.shape[2]
    strip_h = image.shape[3]
    gscale = GRAD_COEF / math.sqrt(
        lax.axis_size("space") * lax.axis_size("slide") * strip_w * strip_h
    )
    live_tiles = tissue[0]
    pixel_mask = jnp.repeat(jnp.repeat(live_tiles, TP, axis=0), TP, axis=1).astype(jnp.bfloat16)
    pix_f = pixel_mask[None].astype(flt)
    masked = image[0] * pixel_mask[None]
    rimmed = extended(masked, (("space", 1),), RADIUS)
    padded = jnp.pad(rimmed, ((0, 0), (0, 0), (RADIUS, RADIUS)))
    pre = depthwise(padded, dw_kernel, strip_w, strip_h) + dw_bias[:, None, None]
    centered = pre - jnp.mean(pre, axis=0, keepdims=True)
    inv_std = lax.rsqrt(jnp.mean(centered * centered, axis=0, keepdims=True) + EPSILON)
    normed = centered * inv_std
    ln_out = rounded(normed * ln_gain[:, None, None] + ln_bias[:, None, None])
    cot_f = cotangent[0].astype(flt)
    grad_mix = rounded(cot_f * pix_f * layer_scale[:, None, None])
    channels, pixels = ln_out.shape[0], strip_w * strip_h
    mo_flat, dxh_flat, gw_in, gw_out, gb_in, gb_out = mlp_pixels(
        w_in, w_out, b_in, b_out, ln_out.reshape(channels, pixels), grad_mix.reshape(channels, pixels)
    )
    mlp_out = mo_flat.reshape(ln_out.shape) * pixel_mask[None]
    grad_ln = dxh_flat.reshape(ln_out.shape) * pixel_mask[None]
    out_image = (
        pix_f * (masked.astype(flt) + layer_scale[:, None, None] * mlp_out.astype(flt))
    ).astype(jnp.bfloat16)
    q_term = grad_ln.astype(flt) * ln_gain[:, None, None]
    grad_pre = rounded(
        inv_std
        * (
            q_term
            - jnp.mean(q_term, axis=0, keepdims=True)
            - normed * jnp.mean(q_term * normed, axis=0, keepdims=True)
        )
    )
    grad_rim = extended(grad_pre, (("space", 1),), RADIUS)
    grad_padded = jnp.pad(grad_rim, ((0, 0), (0, 0), (RADIUS, RADIUS)))
    back_conv = depthwise(grad_padded, dw_kernel[:, ::-1], strip_w, strip_h)
    grad_image = (pix_f * (cot_f + back_conv)).astype(jnp.bfloat16)
    grad_k = kernel_sums(padded, grad_pre, strip_w, strip_h) * gscale
    vectors = (
        jnp.stack(
            [
                jnp.sum(grad_pre.astype(flt), axis=(1, 2)),
                jnp.sum(grad_ln.astype(flt) * normed, axis=(1, 2)),
                jnp.sum(grad_ln.astype(flt), axis=(1, 2)),
                gb_out,
                jnp.sum(cot_f * pix_f * mlp_out.astype(flt), axis=(1, 2)),
            ],
            axis=0,
        )
        * gscale
    )
    local_mlp = jnp.stack([gw_in, gw_out], axis=0) * gscale
    grad_mlp, grad_kernel, grad_vectors, grad_b_in = summed_everywhere(
        (local_mlp, grad_k, vectors, gb_in * gscale), ("space", "slide")
    )
    return (out_image[None], grad_image[None], grad_mlp, grad_kernel, grad_vectors, grad_b_in)


def solution(mesh):
    placed = (
        P("slide", None, "space", None),
        P("slide", None, "space", None),
        P("slide", "space", None),
        P(),
        P(),
        P(),
        P(),
        P(),
        P(),
        P(),
        P(),
        P(),
    )
    return jax.shard_map(
        on_device,
        mesh=mesh,
        in_specs=placed,
        out_specs=(
            P("slide", None, "space", None),
            P("slide", None, "space", None),
            P(),
            P(),
            P(),
            P(),
        ),
        check_vma=False,
    )
```

```python
import math

import jax
import jax.numpy as jnp
from jax import lax
from jax.sharding import PartitionSpec as P

TP = 16
TROWS = 8
TCOL_DEV = 1
MOST = 8


RADIUS = 3
KERNEL_SIDE = 7
EPSILON = 1e-06
GRAD_COEF = 4.0


def extended(block, sides, width):
    for axis, dim in sides:
        count = lax.axis_size(axis)
        forward = [(i, i + 1) for i in range(count - 1)]
        backward = [(target, source) for source, target in forward]
        low = lax.ppermute(
            lax.slice_in_dim(block, block.shape[dim] - width, None, axis=dim), axis, forward
        )
        high = lax.ppermute(lax.slice_in_dim(block, 0, width, axis=dim), axis, backward)
        block = jnp.concatenate([low, block, high], axis=dim)
    return block


def shifted(values, axis, stride, radix, shift):
    pairs = []
    for i in range(lax.axis_size(axis)):
        digit = (i // stride) % radix
        pairs.append((i, i + ((digit + shift) % radix - digit) * stride))
    return lax.ppermute(values, axis, pairs)


def digit_groups(axes):
    groups = []
    for axis in axes:
        stride, size = 1, lax.axis_size(axis)
        while stride < size:
            radix = 4 if size % (stride * 4) == 0 else 2
            groups.append((axis, stride, radix))
            stride *= radix
    return groups


def summed_everywhere(parts, axes, lanes=128):
    flat = jnp.concatenate([p.reshape(-1) for p in parts])
    rows = -(-flat.shape[0] // lanes)
    rows += (-rows) % 128
    block = jnp.pad(flat, (0, rows * lanes - flat.shape[0])).reshape(rows, lanes)
    steps = []
    for axis, stride, radix in digit_groups(axes):
        digit = (lax.axis_index(axis) // stride) % radix
        height, rest = divmod(block.shape[0], radix)
        if rest:
            stack = jnp.zeros((radix,) + block.shape, block.dtype)
            stack = lax.dynamic_update_index_in_dim(stack, block, digit, 0)
            for shift in range(1, radix):
                got = shifted(block, axis, stride, radix, shift)
                stack = lax.dynamic_update_index_in_dim(stack, got, (digit - shift) % radix, 0)
            block = stack[0]
            for k in range(1, radix):
                block = block + stack[k]
            continue
        keep = lax.dynamic_slice_in_dim(block, digit * height, height)
        for shift in range(1, radix):
            send = lax.dynamic_slice_in_dim(block, ((digit + shift) % radix) * height, height)
            keep = keep + shifted(send, axis, stride, radix, shift)
        block = keep
        steps.append((axis, stride, radix, digit))
    for axis, stride, radix, digit in reversed(steps):
        height = block.shape[0]
        whole = jnp.zeros((height * radix,) + block.shape[1:], block.dtype)
        whole = lax.dynamic_update_slice_in_dim(whole, block, digit * height, 0)
        for shift in range(1, radix):
            got = shifted(block, axis, stride, radix, shift)
            whole = lax.dynamic_update_slice_in_dim(
                whole, got, ((digit - shift) % radix) * height, 0
            )
        block = whole
    flat = block.reshape(-1)
    out, start = [], 0
    for p in parts:
        out.append(flat[start : start + p.size].reshape(p.shape))
        start += p.size
    return tuple(out)

def values_bf16(values):
    return values.astype(jnp.bfloat16)


def rounded(values):
    return lax.optimization_barrier(values.astype(jnp.bfloat16))


def gelu_value(values):
    return 0.5 * values * (1.0 + jax.scipy.special.erf(values * (1.0 / math.sqrt(2.0))))


def gelu_slope(values):
    return 0.5 * (1.0 + jax.scipy.special.erf(values * (1.0 / math.sqrt(2.0)))) + values * jnp.exp(
        -0.5 * values * values
    ) * (1.0 / math.sqrt(2.0 * math.pi))


def depthwise(padded, kernel, strip_w, strip_h):
    result = jnp.zeros((padded.shape[0], strip_w, strip_h), jnp.float32)
    for k_row in range(KERNEL_SIDE):
        for k_col in range(KERNEL_SIDE):
            weight = kernel[:, k_row * KERNEL_SIDE + k_col][:, None, None]
            result = result + weight * padded[
                :, k_row : k_row + strip_w, k_col : k_col + strip_h
            ].astype(jnp.float32)
    return result


def kernel_sums(padded, grad_pre, strip_w, strip_h):
    grad_f = grad_pre.astype(jnp.float32)
    entries = []
    for k_row in range(KERNEL_SIDE):
        for k_col in range(KERNEL_SIDE):
            piece = padded[:, k_row : k_row + strip_w, k_col : k_col + strip_h].astype(jnp.float32)
            entries.append(jnp.sum(grad_f * piece, axis=(1, 2)))
    return jnp.stack(entries, axis=1)


def to_tiles(planes):
    channels = planes.shape[0]
    shaped = planes.reshape(channels, TCOL_DEV, TP, TROWS, TP).transpose(1, 3, 0, 2, 4)
    return shaped.reshape(TCOL_DEV * TROWS, channels, TP * TP)


def from_tiles(tiles_in):
    channels = tiles_in.shape[1]
    shaped = tiles_in.reshape(TCOL_DEV, TROWS, channels, TP, TP).transpose(2, 0, 3, 1, 4)
    return shaped.reshape(channels, TCOL_DEV * TP, TROWS * TP)


def mlp_pixels(w_in, w_out, b_in, b_out, x_pix, d_pix):
    flt = jnp.float32
    pre_act = jnp.einsum("cf,cp->fp", w_in, x_pix, preferred_element_type=flt) + b_in[:, None]
    hidden = values_bf16(gelu_value(pre_act))
    mlp_out = values_bf16(
        jnp.einsum("cf,fp->cp", w_out, hidden, preferred_element_type=flt) + b_out[:, None]
    )
    back_hid = jnp.einsum("cf,cp->fp", w_out, d_pix, preferred_element_type=flt)
    grad_act = values_bf16(back_hid * gelu_slope(pre_act))
    grad_ln = values_bf16(jnp.einsum("cf,fp->cp", w_in, grad_act, preferred_element_type=flt))
    gw_in = jnp.einsum("cp,fp->cf", x_pix, grad_act, preferred_element_type=flt)
    gw_out = jnp.einsum("cp,fp->cf", d_pix, hidden, preferred_element_type=flt)
    gb_in = jnp.sum(grad_act.astype(flt), axis=1)
    gb_out = jnp.sum(d_pix.astype(flt), axis=1)
    return (mlp_out, grad_ln, gw_in, gw_out, gb_in, gb_out)


def on_device(
    image,
    cotangent,
    tissue,
    dw_kernel,
    dw_bias,
    ln_gain,
    ln_bias,
    w_in,
    b_in,
    w_out,
    b_out,
    layer_scale,
):
    flt = jnp.float32
    strip_w = image.shape[2]
    strip_h = image.shape[3]
    gscale = GRAD_COEF / math.sqrt(
        lax.axis_size("space") * lax.axis_size("slide") * strip_w * strip_h
    )
    live_tiles = tissue[0]
    pixel_mask = jnp.repeat(jnp.repeat(live_tiles, TP, axis=0), TP, axis=1).astype(jnp.bfloat16)
    pix_f = pixel_mask[None].astype(flt)
    masked = image[0] * pixel_mask[None]
    rimmed = extended(masked, (("space", 1),), RADIUS)
    padded = jnp.pad(rimmed, ((0, 0), (0, 0), (RADIUS, RADIUS)))
    pre = depthwise(padded, dw_kernel, strip_w, strip_h) + dw_bias[:, None, None]
    centered = pre - jnp.mean(pre, axis=0, keepdims=True)
    inv_std = lax.rsqrt(jnp.mean(centered * centered, axis=0, keepdims=True) + EPSILON)
    normed = centered * inv_std
    ln_out = rounded(normed * ln_gain[:, None, None] + ln_bias[:, None, None])
    cot_f = cotangent[0].astype(flt)
    grad_mix = rounded(cot_f * pix_f * layer_scale[:, None, None])
    channels, pixels = ln_out.shape[0], strip_w * strip_h
    mo_flat, dxh_flat, gw_in, gw_out, gb_in, gb_out = mlp_pixels(
        w_in, w_out, b_in, b_out, ln_out.reshape(channels, pixels), grad_mix.reshape(channels, pixels)
    )
    mlp_out = mo_flat.reshape(ln_out.shape) * pixel_mask[None]
    grad_ln = dxh_flat.reshape(ln_out.shape) * pixel_mask[None]
    out_image = (
        pix_f * (masked.astype(flt) + layer_scale[:, None, None] * mlp_out.astype(flt))
    ).astype(jnp.bfloat16)
    q_term = grad_ln.astype(flt) * ln_gain[:, None, None]
    grad_pre = rounded(
        inv_std
        * (
            q_term
            - jnp.mean(q_term, axis=0, keepdims=True)
            - normed * jnp.mean(q_term * normed, axis=0, keepdims=True)
        )
    )
    grad_rim = extended(grad_pre, (("space", 1),), RADIUS)
    grad_padded = jnp.pad(grad_rim, ((0, 0), (0, 0), (RADIUS, RADIUS)))
    back_conv = depthwise(grad_padded, dw_kernel[:, ::-1], strip_w, strip_h)
    grad_image = (pix_f * (cot_f + back_conv)).astype(jnp.bfloat16)
    grad_k = kernel_sums(padded, grad_pre, strip_w, strip_h) * gscale
    vectors = (
        jnp.stack(
            [
                jnp.sum(grad_pre.astype(flt), axis=(1, 2)),
                jnp.sum(grad_ln.astype(flt) * normed, axis=(1, 2)),
                jnp.sum(grad_ln.astype(flt), axis=(1, 2)),
                gb_out,
                jnp.sum(cot_f * pix_f * mlp_out.astype(flt), axis=(1, 2)),
            ],
            axis=0,
        )
        * gscale
    )
    local_mlp = jnp.stack([gw_in, gw_out], axis=0) * gscale
    grad_mlp, grad_kernel, grad_vectors, grad_b_in = summed_everywhere(
        (local_mlp, grad_k, vectors, gb_in * gscale), ("space", "slide")
    )
    return (out_image[None], grad_image[None], grad_mlp, grad_kernel, grad_vectors, grad_b_in)


def solution(mesh):
    placed = (
        P("slide", None, "space", None),
        P("slide", None, "space", None),
        P("slide", "space", None),
        P(),
        P(),
        P(),
        P(),
        P(),
        P(),
        P(),
        P(),
        P(),
    )
    return jax.shard_map(
        on_device,
        mesh=mesh,
        in_specs=placed,
        out_specs=(
            P("slide", None, "space", None),
            P("slide", None, "space", None),
            P(),
            P(),
            P(),
            P(),
        ),
        check_vma=False,
    )
```

```python
import math

import jax
import jax.numpy as jnp
from jax import lax
from jax.sharding import PartitionSpec as P

TP = 16
TROWS = 8
TCOL_DEV = 1
MOST = 8


RADIUS = 3
KERNEL_SIDE = 7
EPSILON = 1e-06
GRAD_COEF = 4.0


def extended(block, sides, width):
    for axis, dim in sides:
        count = lax.axis_size(axis)
        forward = [(i, i + 1) for i in range(count - 1)]
        backward = [(target, source) for source, target in forward]
        low = lax.ppermute(
            lax.slice_in_dim(block, block.shape[dim] - width, None, axis=dim), axis, forward
        )
        high = lax.ppermute(lax.slice_in_dim(block, 0, width, axis=dim), axis, backward)
        block = jnp.concatenate([low, block, high], axis=dim)
    return block


def shifted(values, axis, stride, radix, shift):
    pairs = []
    for i in range(lax.axis_size(axis)):
        digit = (i // stride) % radix
        pairs.append((i, i + ((digit + shift) % radix - digit) * stride))
    return lax.ppermute(values, axis, pairs)


def digit_groups(axes):
    groups = []
    for axis in axes:
        stride, size = 1, lax.axis_size(axis)
        while stride < size:
            radix = 4 if size % (stride * 4) == 0 else 2
            groups.append((axis, stride, radix))
            stride *= radix
    return groups


def summed_everywhere(parts, axes, lanes=128, halvings=2):
    flat = jnp.concatenate([p.reshape(-1) for p in parts])
    rows = -(-flat.shape[0] // lanes)
    rows += (-rows) % 128
    block = jnp.pad(flat, (0, rows * lanes - flat.shape[0])).reshape(rows, lanes)
    steps = []
    for number, (axis, stride, radix) in enumerate(digit_groups(axes)):
        digit = (lax.axis_index(axis) // stride) % radix
        height, rest = divmod(block.shape[0], radix)
        if rest or number >= halvings:
            stack = jnp.zeros((radix,) + block.shape, block.dtype)
            stack = lax.dynamic_update_index_in_dim(stack, block, digit, 0)
            for shift in range(1, radix):
                got = shifted(block, axis, stride, radix, shift)
                stack = lax.dynamic_update_index_in_dim(stack, got, (digit - shift) % radix, 0)
            block = stack[0]
            for k in range(1, radix):
                block = block + stack[k]
            continue
        keep = lax.dynamic_slice_in_dim(block, digit * height, height)
        for shift in range(1, radix):
            send = lax.dynamic_slice_in_dim(block, ((digit + shift) % radix) * height, height)
            keep = keep + shifted(send, axis, stride, radix, shift)
        block = keep
        steps.append((axis, stride, radix, digit))
    for axis, stride, radix, digit in reversed(steps):
        height = block.shape[0]
        whole = jnp.zeros((height * radix,) + block.shape[1:], block.dtype)
        whole = lax.dynamic_update_slice_in_dim(whole, block, digit * height, 0)
        for shift in range(1, radix):
            got = shifted(block, axis, stride, radix, shift)
            whole = lax.dynamic_update_slice_in_dim(
                whole, got, ((digit - shift) % radix) * height, 0
            )
        block = whole
    flat = block.reshape(-1)
    out, start = [], 0
    for p in parts:
        out.append(flat[start : start + p.size].reshape(p.shape))
        start += p.size
    return tuple(out)

def rounded(values):
    return lax.optimization_barrier(values.astype(jnp.bfloat16))


def gelu_value(values):
    return 0.5 * values * (1.0 + jax.scipy.special.erf(values * (1.0 / math.sqrt(2.0))))


def gelu_slope(values):
    return 0.5 * (1.0 + jax.scipy.special.erf(values * (1.0 / math.sqrt(2.0)))) + values * jnp.exp(
        -0.5 * values * values
    ) * (1.0 / math.sqrt(2.0 * math.pi))


def depthwise(padded, kernel, strip_w, strip_h):
    result = jnp.zeros((padded.shape[0], strip_w, strip_h), jnp.float32)
    for k_row in range(KERNEL_SIDE):
        for k_col in range(KERNEL_SIDE):
            weight = kernel[:, k_row * KERNEL_SIDE + k_col][:, None, None]
            result = result + weight * padded[
                :, k_row : k_row + strip_w, k_col : k_col + strip_h
            ].astype(jnp.float32)
    return result


def kernel_sums(padded, grad_pre, strip_w, strip_h):
    grad_f = grad_pre.astype(jnp.float32)
    entries = []
    for k_row in range(KERNEL_SIDE):
        for k_col in range(KERNEL_SIDE):
            piece = padded[:, k_row : k_row + strip_w, k_col : k_col + strip_h].astype(jnp.float32)
            entries.append(jnp.sum(grad_f * piece, axis=(1, 2)))
    return jnp.stack(entries, axis=1)


def to_tiles(planes):
    channels = planes.shape[0]
    shaped = planes.reshape(channels, TCOL_DEV, TP, TROWS, TP).transpose(1, 3, 0, 2, 4)
    return shaped.reshape(TCOL_DEV * TROWS, channels, TP * TP)


def from_tiles(tiles_in):
    channels = tiles_in.shape[1]
    shaped = tiles_in.reshape(TCOL_DEV, TROWS, channels, TP, TP).transpose(2, 0, 3, 1, 4)
    return shaped.reshape(channels, TCOL_DEV * TP, TROWS * TP)


def mlp_pixels(w_in, w_out, b_in, b_out, x_pix, d_pix):
    flt = jnp.float32
    pre_act = jnp.einsum("cf,cp->fp", w_in, x_pix, preferred_element_type=flt) + b_in[:, None]
    hidden = rounded(gelu_value(pre_act))
    mlp_out = rounded(
        jnp.einsum("cf,fp->cp", w_out, hidden, preferred_element_type=flt) + b_out[:, None]
    )
    back_hid = jnp.einsum("cf,cp->fp", w_out, d_pix, preferred_element_type=flt)
    grad_act = rounded(back_hid * gelu_slope(pre_act))
    grad_ln = rounded(jnp.einsum("cf,fp->cp", w_in, grad_act, preferred_element_type=flt))
    gw_in = jnp.einsum("cp,fp->cf", x_pix, grad_act, preferred_element_type=flt)
    gw_out = jnp.einsum("cp,fp->cf", d_pix, hidden, preferred_element_type=flt)
    gb_in = jnp.sum(grad_act.astype(flt), axis=1)
    gb_out = jnp.sum(d_pix.astype(flt), axis=1)
    return (mlp_out, grad_ln, gw_in, gw_out, gb_in, gb_out)


def on_device(
    image,
    cotangent,
    tissue,
    dw_kernel,
    dw_bias,
    ln_gain,
    ln_bias,
    w_in,
    b_in,
    w_out,
    b_out,
    layer_scale,
):
    flt = jnp.float32
    strip_w = image.shape[2]
    strip_h = image.shape[3]
    gscale = GRAD_COEF / math.sqrt(
        lax.axis_size("space") * lax.axis_size("slide") * strip_w * strip_h
    )
    live_tiles = tissue[0]
    pixel_mask = jnp.repeat(jnp.repeat(live_tiles, TP, axis=0), TP, axis=1).astype(jnp.bfloat16)
    pix_f = pixel_mask[None].astype(flt)
    masked = image[0] * pixel_mask[None]
    rimmed = extended(masked, (("space", 1),), RADIUS)
    padded = jnp.pad(rimmed, ((0, 0), (0, 0), (RADIUS, RADIUS)))
    pre = depthwise(padded, dw_kernel, strip_w, strip_h) + dw_bias[:, None, None]
    centered = pre - jnp.mean(pre, axis=0, keepdims=True)
    inv_std = lax.rsqrt(jnp.mean(centered * centered, axis=0, keepdims=True) + EPSILON)
    normed = centered * inv_std
    ln_out = rounded(normed * ln_gain[:, None, None] + ln_bias[:, None, None])
    cot_f = cotangent[0].astype(flt)
    grad_mix = rounded(cot_f * pix_f * layer_scale[:, None, None])
    channels, pixels = ln_out.shape[0], strip_w * strip_h
    mo_flat, dxh_flat, gw_in, gw_out, gb_in, gb_out = mlp_pixels(
        w_in, w_out, b_in, b_out, ln_out.reshape(channels, pixels), grad_mix.reshape(channels, pixels)
    )
    mlp_out = mo_flat.reshape(ln_out.shape) * pixel_mask[None]
    grad_ln = dxh_flat.reshape(ln_out.shape) * pixel_mask[None]
    out_image = (
        pix_f * (masked.astype(flt) + layer_scale[:, None, None] * mlp_out.astype(flt))
    ).astype(jnp.bfloat16)
    q_term = grad_ln.astype(flt) * ln_gain[:, None, None]
    grad_pre = rounded(
        inv_std
        * (
            q_term
            - jnp.mean(q_term, axis=0, keepdims=True)
            - normed * jnp.mean(q_term * normed, axis=0, keepdims=True)
        )
    )
    grad_rim = extended(grad_pre, (("space", 1),), RADIUS)
    grad_padded = jnp.pad(grad_rim, ((0, 0), (0, 0), (RADIUS, RADIUS)))
    back_conv = depthwise(grad_padded, dw_kernel[:, ::-1], strip_w, strip_h)
    grad_image = (pix_f * (cot_f + back_conv)).astype(jnp.bfloat16)
    grad_k = kernel_sums(padded, grad_pre, strip_w, strip_h) * gscale
    vectors = (
        jnp.stack(
            [
                jnp.sum(grad_pre.astype(flt), axis=(1, 2)),
                jnp.sum(grad_ln.astype(flt) * normed, axis=(1, 2)),
                jnp.sum(grad_ln.astype(flt), axis=(1, 2)),
                gb_out,
                jnp.sum(cot_f * pix_f * mlp_out.astype(flt), axis=(1, 2)),
            ],
            axis=0,
        )
        * gscale
    )
    local_mlp = jnp.stack([gw_in, gw_out], axis=0) * gscale
    grad_mlp, grad_kernel, grad_vectors, grad_b_in = summed_everywhere(
        (local_mlp, grad_k, vectors, gb_in * gscale), ("space", "slide")
    )
    return (out_image[None], grad_image[None], grad_mlp, grad_kernel, grad_vectors, grad_b_in)


def solution(mesh):
    placed = (
        P("slide", None, "space", None),
        P("slide", None, "space", None),
        P("slide", "space", None),
        P(),
        P(),
        P(),
        P(),
        P(),
        P(),
        P(),
        P(),
        P(),
    )
    return jax.shard_map(
        on_device,
        mesh=mesh,
        in_specs=placed,
        out_specs=(
            P("slide", None, "space", None),
            P("slide", None, "space", None),
            P(),
            P(),
            P(),
            P(),
        ),
        check_vma=False,
    )
```

```python
import math

import jax
import jax.numpy as jnp
from jax import lax
from jax.sharding import PartitionSpec as P

TP = 16
TROWS = 8
TCOL_DEV = 1
MOST = 8


RADIUS = 3
KERNEL_SIDE = 7
EPSILON = 1e-06
GRAD_COEF = 4.0


def extended(block, sides, width):
    for axis, dim in sides:
        count = lax.axis_size(axis)
        forward = [(i, i + 1) for i in range(count - 1)]
        backward = [(target, source) for source, target in forward]
        low = lax.ppermute(
            lax.slice_in_dim(block, block.shape[dim] - width, None, axis=dim), axis, forward
        )
        high = lax.ppermute(lax.slice_in_dim(block, 0, width, axis=dim), axis, backward)
        block = jnp.concatenate([low, block, high], axis=dim)
    return block


def shifted(values, axis, stride, radix, shift):
    pairs = []
    for i in range(lax.axis_size(axis)):
        digit = (i // stride) % radix
        pairs.append((i, i + ((digit + shift) % radix - digit) * stride))
    return lax.ppermute(values, axis, pairs)


def digit_groups(axes):
    groups = []
    for axis in axes:
        stride, size = 1, lax.axis_size(axis)
        while stride < size:
            radix = 4 if size % (stride * 4) == 0 else 2
            groups.append((axis, stride, radix))
            stride *= radix
    return groups


def summed_everywhere(parts, axes, lanes=128, halvings=1):
    flat = jnp.concatenate([p.reshape(-1) for p in parts])
    rows = -(-flat.shape[0] // lanes)
    rows += (-rows) % 128
    block = jnp.pad(flat, (0, rows * lanes - flat.shape[0])).reshape(rows, lanes)
    steps = []
    for number, (axis, stride, radix) in enumerate(digit_groups(axes)):
        digit = (lax.axis_index(axis) // stride) % radix
        height, rest = divmod(block.shape[0], radix)
        if rest or number >= halvings:
            stack = jnp.zeros((radix,) + block.shape, block.dtype)
            stack = lax.dynamic_update_index_in_dim(stack, block, digit, 0)
            for shift in range(1, radix):
                got = shifted(block, axis, stride, radix, shift)
                stack = lax.dynamic_update_index_in_dim(stack, got, (digit - shift) % radix, 0)
            block = stack[0]
            for k in range(1, radix):
                block = block + stack[k]
            continue
        keep = lax.dynamic_slice_in_dim(block, digit * height, height)
        for shift in range(1, radix):
            send = lax.dynamic_slice_in_dim(block, ((digit + shift) % radix) * height, height)
            keep = keep + shifted(send, axis, stride, radix, shift)
        block = keep
        steps.append((axis, stride, radix, digit))
    for axis, stride, radix, digit in reversed(steps):
        height = block.shape[0]
        whole = jnp.zeros((height * radix,) + block.shape[1:], block.dtype)
        whole = lax.dynamic_update_slice_in_dim(whole, block, digit * height, 0)
        for shift in range(1, radix):
            got = shifted(block, axis, stride, radix, shift)
            whole = lax.dynamic_update_slice_in_dim(
                whole, got, ((digit - shift) % radix) * height, 0
            )
        block = whole
    flat = block.reshape(-1)
    out, start = [], 0
    for p in parts:
        out.append(flat[start : start + p.size].reshape(p.shape))
        start += p.size
    return tuple(out)

def rounded(values):
    return lax.optimization_barrier(values.astype(jnp.bfloat16))


def gelu_value(values):
    return 0.5 * values * (1.0 + jax.scipy.special.erf(values * (1.0 / math.sqrt(2.0))))


def gelu_slope(values):
    return 0.5 * (1.0 + jax.scipy.special.erf(values * (1.0 / math.sqrt(2.0)))) + values * jnp.exp(
        -0.5 * values * values
    ) * (1.0 / math.sqrt(2.0 * math.pi))


def depthwise(padded, kernel, strip_w, strip_h):
    result = jnp.zeros((padded.shape[0], strip_w, strip_h), jnp.float32)
    for k_row in range(KERNEL_SIDE):
        for k_col in range(KERNEL_SIDE):
            weight = kernel[:, k_row * KERNEL_SIDE + k_col][:, None, None]
            result = result + weight * padded[
                :, k_row : k_row + strip_w, k_col : k_col + strip_h
            ].astype(jnp.float32)
    return result


def kernel_sums(padded, grad_pre, strip_w, strip_h):
    grad_f = grad_pre.astype(jnp.float32)
    entries = []
    for k_row in range(KERNEL_SIDE):
        for k_col in range(KERNEL_SIDE):
            piece = padded[:, k_row : k_row + strip_w, k_col : k_col + strip_h].astype(jnp.float32)
            entries.append(jnp.sum(grad_f * piece, axis=(1, 2)))
    return jnp.stack(entries, axis=1)


def to_tiles(planes):
    channels = planes.shape[0]
    shaped = planes.reshape(channels, TCOL_DEV, TP, TROWS, TP).transpose(1, 3, 0, 2, 4)
    return shaped.reshape(TCOL_DEV * TROWS, channels, TP * TP)


def from_tiles(tiles_in):
    channels = tiles_in.shape[1]
    shaped = tiles_in.reshape(TCOL_DEV, TROWS, channels, TP, TP).transpose(2, 0, 3, 1, 4)
    return shaped.reshape(channels, TCOL_DEV * TP, TROWS * TP)


def mlp_pixels(w_in, w_out, b_in, b_out, x_pix, d_pix):
    flt = jnp.float32
    pre_act = jnp.einsum("cf,cp->fp", w_in, x_pix, preferred_element_type=flt) + b_in[:, None]
    hidden = rounded(gelu_value(pre_act))
    mlp_out = rounded(
        jnp.einsum("cf,fp->cp", w_out, hidden, preferred_element_type=flt) + b_out[:, None]
    )
    back_hid = jnp.einsum("cf,cp->fp", w_out, d_pix, preferred_element_type=flt)
    grad_act = rounded(back_hid * gelu_slope(pre_act))
    grad_ln = rounded(jnp.einsum("cf,fp->cp", w_in, grad_act, preferred_element_type=flt))
    gw_in = jnp.einsum("cp,fp->cf", x_pix, grad_act, preferred_element_type=flt)
    gw_out = jnp.einsum("cp,fp->cf", d_pix, hidden, preferred_element_type=flt)
    gb_in = jnp.sum(grad_act.astype(flt), axis=1)
    gb_out = jnp.sum(d_pix.astype(flt), axis=1)
    return (mlp_out, grad_ln, gw_in, gw_out, gb_in, gb_out)


def on_device(
    image,
    cotangent,
    tissue,
    dw_kernel,
    dw_bias,
    ln_gain,
    ln_bias,
    w_in,
    b_in,
    w_out,
    b_out,
    layer_scale,
):
    flt = jnp.float32
    strip_w = image.shape[2]
    strip_h = image.shape[3]
    gscale = GRAD_COEF / math.sqrt(
        lax.axis_size("space") * lax.axis_size("slide") * strip_w * strip_h
    )
    live_tiles = tissue[0]
    pixel_mask = jnp.repeat(jnp.repeat(live_tiles, TP, axis=0), TP, axis=1).astype(jnp.bfloat16)
    pix_f = pixel_mask[None].astype(flt)
    masked = image[0] * pixel_mask[None]
    rimmed = extended(masked, (("space", 1),), RADIUS)
    padded = jnp.pad(rimmed, ((0, 0), (0, 0), (RADIUS, RADIUS)))
    pre = depthwise(padded, dw_kernel, strip_w, strip_h) + dw_bias[:, None, None]
    centered = pre - jnp.mean(pre, axis=0, keepdims=True)
    inv_std = lax.rsqrt(jnp.mean(centered * centered, axis=0, keepdims=True) + EPSILON)
    normed = centered * inv_std
    ln_out = rounded(normed * ln_gain[:, None, None] + ln_bias[:, None, None])
    cot_f = cotangent[0].astype(flt)
    grad_mix = rounded(cot_f * pix_f * layer_scale[:, None, None])
    channels, pixels = ln_out.shape[0], strip_w * strip_h
    mo_flat, dxh_flat, gw_in, gw_out, gb_in, gb_out = mlp_pixels(
        w_in, w_out, b_in, b_out, ln_out.reshape(channels, pixels), grad_mix.reshape(channels, pixels)
    )
    mlp_out = mo_flat.reshape(ln_out.shape) * pixel_mask[None]
    grad_ln = dxh_flat.reshape(ln_out.shape) * pixel_mask[None]
    out_image = (
        pix_f * (masked.astype(flt) + layer_scale[:, None, None] * mlp_out.astype(flt))
    ).astype(jnp.bfloat16)
    q_term = grad_ln.astype(flt) * ln_gain[:, None, None]
    grad_pre = rounded(
        inv_std
        * (
            q_term
            - jnp.mean(q_term, axis=0, keepdims=True)
            - normed * jnp.mean(q_term * normed, axis=0, keepdims=True)
        )
    )
    grad_rim = extended(grad_pre, (("space", 1),), RADIUS)
    grad_padded = jnp.pad(grad_rim, ((0, 0), (0, 0), (RADIUS, RADIUS)))
    back_conv = depthwise(grad_padded, dw_kernel[:, ::-1], strip_w, strip_h)
    grad_image = (pix_f * (cot_f + back_conv)).astype(jnp.bfloat16)
    grad_k = kernel_sums(padded, grad_pre, strip_w, strip_h) * gscale
    vectors = (
        jnp.stack(
            [
                jnp.sum(grad_pre.astype(flt), axis=(1, 2)),
                jnp.sum(grad_ln.astype(flt) * normed, axis=(1, 2)),
                jnp.sum(grad_ln.astype(flt), axis=(1, 2)),
                gb_out,
                jnp.sum(cot_f * pix_f * mlp_out.astype(flt), axis=(1, 2)),
            ],
            axis=0,
        )
        * gscale
    )
    local_mlp = jnp.stack([gw_in, gw_out], axis=0) * gscale
    grad_mlp, grad_kernel, grad_vectors, grad_b_in = summed_everywhere(
        (local_mlp, grad_k, vectors, gb_in * gscale), ("space", "slide")
    )
    return (out_image[None], grad_image[None], grad_mlp, grad_kernel, grad_vectors, grad_b_in)


def solution(mesh):
    placed = (
        P("slide", None, "space", None),
        P("slide", None, "space", None),
        P("slide", "space", None),
        P(),
        P(),
        P(),
        P(),
        P(),
        P(),
        P(),
        P(),
        P(),
    )
    return jax.shard_map(
        on_device,
        mesh=mesh,
        in_specs=placed,
        out_specs=(
            P("slide", None, "space", None),
            P("slide", None, "space", None),
            P(),
            P(),
            P(),
            P(),
        ),
        check_vma=False,
    )
```

```python
import math

import jax
import jax.numpy as jnp
from jax import lax
from jax.sharding import PartitionSpec as P

TP = 16
TROWS = 8
TCOL_DEV = 1
MOST = 8


RADIUS = 3
KERNEL_SIDE = 7
EPSILON = 1e-06
GRAD_COEF = 4.0


def extended(block, sides, width):
    for axis, dim in sides:
        count = lax.axis_size(axis)
        forward = [(i, i + 1) for i in range(count - 1)]
        backward = [(target, source) for source, target in forward]
        low = lax.ppermute(
            lax.slice_in_dim(block, block.shape[dim] - width, None, axis=dim), axis, forward
        )
        high = lax.ppermute(lax.slice_in_dim(block, 0, width, axis=dim), axis, backward)
        block = jnp.concatenate([low, block, high], axis=dim)
    return block


def shifted(values, axis, stride, radix, shift):
    pairs = []
    for i in range(lax.axis_size(axis)):
        digit = (i // stride) % radix
        pairs.append((i, i + ((digit + shift) % radix - digit) * stride))
    return lax.ppermute(values, axis, pairs)


def digit_groups(axes):
    groups = []
    for axis in axes:
        stride, size = 1, lax.axis_size(axis)
        while stride < size:
            radix = 4 if size % (stride * 4) == 0 else 2
            groups.append((axis, stride, radix))
            stride *= radix
    return groups


def summed_everywhere(parts, axes, lanes=128, halvings=0):
    flat = jnp.concatenate([p.reshape(-1) for p in parts])
    rows = -(-flat.shape[0] // lanes)
    rows += (-rows) % 128
    block = jnp.pad(flat, (0, rows * lanes - flat.shape[0])).reshape(rows, lanes)
    steps = []
    for number, (axis, stride, radix) in enumerate(digit_groups(axes)):
        digit = (lax.axis_index(axis) // stride) % radix
        height, rest = divmod(block.shape[0], radix)
        if rest or number >= halvings:
            stack = jnp.zeros((radix,) + block.shape, block.dtype)
            stack = lax.dynamic_update_index_in_dim(stack, block, digit, 0)
            for shift in range(1, radix):
                got = shifted(block, axis, stride, radix, shift)
                stack = lax.dynamic_update_index_in_dim(stack, got, (digit - shift) % radix, 0)
            block = stack[0]
            for k in range(1, radix):
                block = block + stack[k]
            continue
        keep = lax.dynamic_slice_in_dim(block, digit * height, height)
        for shift in range(1, radix):
            send = lax.dynamic_slice_in_dim(block, ((digit + shift) % radix) * height, height)
            keep = keep + shifted(send, axis, stride, radix, shift)
        block = keep
        steps.append((axis, stride, radix, digit))
    for axis, stride, radix, digit in reversed(steps):
        height = block.shape[0]
        whole = jnp.zeros((height * radix,) + block.shape[1:], block.dtype)
        whole = lax.dynamic_update_slice_in_dim(whole, block, digit * height, 0)
        for shift in range(1, radix):
            got = shifted(block, axis, stride, radix, shift)
            whole = lax.dynamic_update_slice_in_dim(
                whole, got, ((digit - shift) % radix) * height, 0
            )
        block = whole
    flat = block.reshape(-1)
    out, start = [], 0
    for p in parts:
        out.append(flat[start : start + p.size].reshape(p.shape))
        start += p.size
    return tuple(out)

def rounded(values):
    return lax.optimization_barrier(values.astype(jnp.bfloat16))


def gelu_value(values):
    return 0.5 * values * (1.0 + jax.scipy.special.erf(values * (1.0 / math.sqrt(2.0))))


def gelu_slope(values):
    return 0.5 * (1.0 + jax.scipy.special.erf(values * (1.0 / math.sqrt(2.0)))) + values * jnp.exp(
        -0.5 * values * values
    ) * (1.0 / math.sqrt(2.0 * math.pi))


def depthwise(padded, kernel, strip_w, strip_h):
    result = jnp.zeros((padded.shape[0], strip_w, strip_h), jnp.float32)
    for k_row in range(KERNEL_SIDE):
        for k_col in range(KERNEL_SIDE):
            weight = kernel[:, k_row * KERNEL_SIDE + k_col][:, None, None]
            result = result + weight * padded[
                :, k_row : k_row + strip_w, k_col : k_col + strip_h
            ].astype(jnp.float32)
    return result


def kernel_sums(padded, grad_pre, strip_w, strip_h):
    grad_f = grad_pre.astype(jnp.float32)
    entries = []
    for k_row in range(KERNEL_SIDE):
        for k_col in range(KERNEL_SIDE):
            piece = padded[:, k_row : k_row + strip_w, k_col : k_col + strip_h].astype(jnp.float32)
            entries.append(jnp.sum(grad_f * piece, axis=(1, 2)))
    return jnp.stack(entries, axis=1)


def to_tiles(planes):
    channels = planes.shape[0]
    shaped = planes.reshape(channels, TCOL_DEV, TP, TROWS, TP).transpose(1, 3, 0, 2, 4)
    return shaped.reshape(TCOL_DEV * TROWS, channels, TP * TP)


def from_tiles(tiles_in):
    channels = tiles_in.shape[1]
    shaped = tiles_in.reshape(TCOL_DEV, TROWS, channels, TP, TP).transpose(2, 0, 3, 1, 4)
    return shaped.reshape(channels, TCOL_DEV * TP, TROWS * TP)


def mlp_pixels(w_in, w_out, b_in, b_out, x_pix, d_pix):
    flt = jnp.float32
    pre_act = jnp.einsum("cf,cp->fp", w_in, x_pix, preferred_element_type=flt) + b_in[:, None]
    hidden = rounded(gelu_value(pre_act))
    mlp_out = rounded(
        jnp.einsum("cf,fp->cp", w_out, hidden, preferred_element_type=flt) + b_out[:, None]
    )
    back_hid = jnp.einsum("cf,cp->fp", w_out, d_pix, preferred_element_type=flt)
    grad_act = rounded(back_hid * gelu_slope(pre_act))
    grad_ln = rounded(jnp.einsum("cf,fp->cp", w_in, grad_act, preferred_element_type=flt))
    gw_in = jnp.einsum("cp,fp->cf", x_pix, grad_act, preferred_element_type=flt)
    gw_out = jnp.einsum("cp,fp->cf", d_pix, hidden, preferred_element_type=flt)
    gb_in = jnp.sum(grad_act.astype(flt), axis=1)
    gb_out = jnp.sum(d_pix.astype(flt), axis=1)
    return (mlp_out, grad_ln, gw_in, gw_out, gb_in, gb_out)


def on_device(
    image,
    cotangent,
    tissue,
    dw_kernel,
    dw_bias,
    ln_gain,
    ln_bias,
    w_in,
    b_in,
    w_out,
    b_out,
    layer_scale,
):
    flt = jnp.float32
    strip_w = image.shape[2]
    strip_h = image.shape[3]
    gscale = GRAD_COEF / math.sqrt(
        lax.axis_size("space") * lax.axis_size("slide") * strip_w * strip_h
    )
    live_tiles = tissue[0]
    pixel_mask = jnp.repeat(jnp.repeat(live_tiles, TP, axis=0), TP, axis=1).astype(jnp.bfloat16)
    pix_f = pixel_mask[None].astype(flt)
    masked = image[0] * pixel_mask[None]
    rimmed = extended(masked, (("space", 1),), RADIUS)
    padded = jnp.pad(rimmed, ((0, 0), (0, 0), (RADIUS, RADIUS)))
    pre = depthwise(padded, dw_kernel, strip_w, strip_h) + dw_bias[:, None, None]
    centered = pre - jnp.mean(pre, axis=0, keepdims=True)
    inv_std = lax.rsqrt(jnp.mean(centered * centered, axis=0, keepdims=True) + EPSILON)
    normed = centered * inv_std
    ln_out = rounded(normed * ln_gain[:, None, None] + ln_bias[:, None, None])
    cot_f = cotangent[0].astype(flt)
    grad_mix = rounded(cot_f * pix_f * layer_scale[:, None, None])
    channels, pixels = ln_out.shape[0], strip_w * strip_h
    mo_flat, dxh_flat, gw_in, gw_out, gb_in, gb_out = mlp_pixels(
        w_in, w_out, b_in, b_out, ln_out.reshape(channels, pixels), grad_mix.reshape(channels, pixels)
    )
    mlp_out = mo_flat.reshape(ln_out.shape) * pixel_mask[None]
    grad_ln = dxh_flat.reshape(ln_out.shape) * pixel_mask[None]
    out_image = (
        pix_f * (masked.astype(flt) + layer_scale[:, None, None] * mlp_out.astype(flt))
    ).astype(jnp.bfloat16)
    q_term = grad_ln.astype(flt) * ln_gain[:, None, None]
    grad_pre = rounded(
        inv_std
        * (
            q_term
            - jnp.mean(q_term, axis=0, keepdims=True)
            - normed * jnp.mean(q_term * normed, axis=0, keepdims=True)
        )
    )
    grad_rim = extended(grad_pre, (("space", 1),), RADIUS)
    grad_padded = jnp.pad(grad_rim, ((0, 0), (0, 0), (RADIUS, RADIUS)))
    back_conv = depthwise(grad_padded, dw_kernel[:, ::-1], strip_w, strip_h)
    grad_image = (pix_f * (cot_f + back_conv)).astype(jnp.bfloat16)
    grad_k = kernel_sums(padded, grad_pre, strip_w, strip_h) * gscale
    vectors = (
        jnp.stack(
            [
                jnp.sum(grad_pre.astype(flt), axis=(1, 2)),
                jnp.sum(grad_ln.astype(flt) * normed, axis=(1, 2)),
                jnp.sum(grad_ln.astype(flt), axis=(1, 2)),
                gb_out,
                jnp.sum(cot_f * pix_f * mlp_out.astype(flt), axis=(1, 2)),
            ],
            axis=0,
        )
        * gscale
    )
    local_mlp = jnp.stack([gw_in, gw_out], axis=0) * gscale
    grad_mlp, grad_kernel, grad_vectors, grad_b_in = summed_everywhere(
        (local_mlp, grad_k, vectors, gb_in * gscale), ("space", "slide")
    )
    return (out_image[None], grad_image[None], grad_mlp, grad_kernel, grad_vectors, grad_b_in)


def solution(mesh):
    placed = (
        P("slide", None, "space", None),
        P("slide", None, "space", None),
        P("slide", "space", None),
        P(),
        P(),
        P(),
        P(),
        P(),
        P(),
        P(),
        P(),
        P(),
    )
    return jax.shard_map(
        on_device,
        mesh=mesh,
        in_specs=placed,
        out_specs=(
            P("slide", None, "space", None),
            P("slide", None, "space", None),
            P(),
            P(),
            P(),
            P(),
        ),
        check_vma=False,
    )
```

```python
import math

import jax
import jax.numpy as jnp
from jax import lax
from jax.sharding import PartitionSpec as P

TP = 16
TROWS = 8
TCOL_DEV = 1
MOST = 8


RADIUS = 3
KERNEL_SIDE = 7
EPSILON = 1e-06
GRAD_COEF = 4.0


def extended(block, sides, width):
    for axis, dim in sides:
        count = lax.axis_size(axis)
        forward = [(i, i + 1) for i in range(count - 1)]
        backward = [(target, source) for source, target in forward]
        low = lax.ppermute(
            lax.slice_in_dim(block, block.shape[dim] - width, None, axis=dim), axis, forward
        )
        high = lax.ppermute(lax.slice_in_dim(block, 0, width, axis=dim), axis, backward)
        block = jnp.concatenate([low, block, high], axis=dim)
    return block


def shifted(values, axis, stride, radix, shift):
    pairs = []
    for i in range(lax.axis_size(axis)):
        digit = (i // stride) % radix
        pairs.append((i, i + ((digit + shift) % radix - digit) * stride))
    return lax.ppermute(values, axis, pairs)


def digit_groups(axes):
    groups = []
    for axis in axes:
        stride, size = 1, lax.axis_size(axis)
        while stride < size:
            radix = 8 if size % (stride * 8) == 0 else 4 if size % (stride * 4) == 0 else 2
            groups.append((axis, stride, radix))
            stride *= radix
    return groups


def summed_everywhere(parts, axes, lanes=128, halvings=1):
    flat = jnp.concatenate([p.reshape(-1) for p in parts])
    rows = -(-flat.shape[0] // lanes)
    rows += (-rows) % 128
    block = jnp.pad(flat, (0, rows * lanes - flat.shape[0])).reshape(rows, lanes)
    steps = []
    for number, (axis, stride, radix) in enumerate(digit_groups(axes)):
        digit = (lax.axis_index(axis) // stride) % radix
        height, rest = divmod(block.shape[0], radix)
        if rest or number >= halvings:
            stack = jnp.zeros((radix,) + block.shape, block.dtype)
            stack = lax.dynamic_update_index_in_dim(stack, block, digit, 0)
            for shift in range(1, radix):
                got = shifted(block, axis, stride, radix, shift)
                stack = lax.dynamic_update_index_in_dim(stack, got, (digit - shift) % radix, 0)
            block = stack[0]
            for k in range(1, radix):
                block = block + stack[k]
            continue
        keep = lax.dynamic_slice_in_dim(block, digit * height, height)
        for shift in range(1, radix):
            send = lax.dynamic_slice_in_dim(block, ((digit + shift) % radix) * height, height)
            keep = keep + shifted(send, axis, stride, radix, shift)
        block = keep
        steps.append((axis, stride, radix, digit))
    for axis, stride, radix, digit in reversed(steps):
        height = block.shape[0]
        whole = jnp.zeros((height * radix,) + block.shape[1:], block.dtype)
        whole = lax.dynamic_update_slice_in_dim(whole, block, digit * height, 0)
        for shift in range(1, radix):
            got = shifted(block, axis, stride, radix, shift)
            whole = lax.dynamic_update_slice_in_dim(
                whole, got, ((digit - shift) % radix) * height, 0
            )
        block = whole
    flat = block.reshape(-1)
    out, start = [], 0
    for p in parts:
        out.append(flat[start : start + p.size].reshape(p.shape))
        start += p.size
    return tuple(out)

def rounded(values):
    return lax.optimization_barrier(values.astype(jnp.bfloat16))


def gelu_value(values):
    return 0.5 * values * (1.0 + jax.scipy.special.erf(values * (1.0 / math.sqrt(2.0))))


def gelu_slope(values):
    return 0.5 * (1.0 + jax.scipy.special.erf(values * (1.0 / math.sqrt(2.0)))) + values * jnp.exp(
        -0.5 * values * values
    ) * (1.0 / math.sqrt(2.0 * math.pi))


def depthwise(padded, kernel, strip_w, strip_h):
    result = jnp.zeros((padded.shape[0], strip_w, strip_h), jnp.float32)
    for k_row in range(KERNEL_SIDE):
        for k_col in range(KERNEL_SIDE):
            weight = kernel[:, k_row * KERNEL_SIDE + k_col][:, None, None]
            result = result + weight * padded[
                :, k_row : k_row + strip_w, k_col : k_col + strip_h
            ].astype(jnp.float32)
    return result


def kernel_sums(padded, grad_pre, strip_w, strip_h):
    grad_f = grad_pre.astype(jnp.float32)
    entries = []
    for k_row in range(KERNEL_SIDE):
        for k_col in range(KERNEL_SIDE):
            piece = padded[:, k_row : k_row + strip_w, k_col : k_col + strip_h].astype(jnp.float32)
            entries.append(jnp.sum(grad_f * piece, axis=(1, 2)))
    return jnp.stack(entries, axis=1)


def to_tiles(planes):
    channels = planes.shape[0]
    shaped = planes.reshape(channels, TCOL_DEV, TP, TROWS, TP).transpose(1, 3, 0, 2, 4)
    return shaped.reshape(TCOL_DEV * TROWS, channels, TP * TP)


def from_tiles(tiles_in):
    channels = tiles_in.shape[1]
    shaped = tiles_in.reshape(TCOL_DEV, TROWS, channels, TP, TP).transpose(2, 0, 3, 1, 4)
    return shaped.reshape(channels, TCOL_DEV * TP, TROWS * TP)


def mlp_pixels(w_in, w_out, b_in, b_out, x_pix, d_pix):
    flt = jnp.float32
    pre_act = jnp.einsum("cf,cp->fp", w_in, x_pix, preferred_element_type=flt) + b_in[:, None]
    hidden = rounded(gelu_value(pre_act))
    mlp_out = rounded(
        jnp.einsum("cf,fp->cp", w_out, hidden, preferred_element_type=flt) + b_out[:, None]
    )
    back_hid = jnp.einsum("cf,cp->fp", w_out, d_pix, preferred_element_type=flt)
    grad_act = rounded(back_hid * gelu_slope(pre_act))
    grad_ln = rounded(jnp.einsum("cf,fp->cp", w_in, grad_act, preferred_element_type=flt))
    gw_in = jnp.einsum("cp,fp->cf", x_pix, grad_act, preferred_element_type=flt)
    gw_out = jnp.einsum("cp,fp->cf", d_pix, hidden, preferred_element_type=flt)
    gb_in = jnp.sum(grad_act.astype(flt), axis=1)
    gb_out = jnp.sum(d_pix.astype(flt), axis=1)
    return (mlp_out, grad_ln, gw_in, gw_out, gb_in, gb_out)


def on_device(
    image,
    cotangent,
    tissue,
    dw_kernel,
    dw_bias,
    ln_gain,
    ln_bias,
    w_in,
    b_in,
    w_out,
    b_out,
    layer_scale,
):
    flt = jnp.float32
    strip_w = image.shape[2]
    strip_h = image.shape[3]
    gscale = GRAD_COEF / math.sqrt(
        lax.axis_size("space") * lax.axis_size("slide") * strip_w * strip_h
    )
    live_tiles = tissue[0]
    pixel_mask = jnp.repeat(jnp.repeat(live_tiles, TP, axis=0), TP, axis=1).astype(jnp.bfloat16)
    pix_f = pixel_mask[None].astype(flt)
    masked = image[0] * pixel_mask[None]
    rimmed = extended(masked, (("space", 1),), RADIUS)
    padded = jnp.pad(rimmed, ((0, 0), (0, 0), (RADIUS, RADIUS)))
    pre = depthwise(padded, dw_kernel, strip_w, strip_h) + dw_bias[:, None, None]
    centered = pre - jnp.mean(pre, axis=0, keepdims=True)
    inv_std = lax.rsqrt(jnp.mean(centered * centered, axis=0, keepdims=True) + EPSILON)
    normed = centered * inv_std
    ln_out = rounded(normed * ln_gain[:, None, None] + ln_bias[:, None, None])
    cot_f = cotangent[0].astype(flt)
    grad_mix = rounded(cot_f * pix_f * layer_scale[:, None, None])
    channels, pixels = ln_out.shape[0], strip_w * strip_h
    mo_flat, dxh_flat, gw_in, gw_out, gb_in, gb_out = mlp_pixels(
        w_in, w_out, b_in, b_out, ln_out.reshape(channels, pixels), grad_mix.reshape(channels, pixels)
    )
    mlp_out = mo_flat.reshape(ln_out.shape) * pixel_mask[None]
    grad_ln = dxh_flat.reshape(ln_out.shape) * pixel_mask[None]
    out_image = (
        pix_f * (masked.astype(flt) + layer_scale[:, None, None] * mlp_out.astype(flt))
    ).astype(jnp.bfloat16)
    q_term = grad_ln.astype(flt) * ln_gain[:, None, None]
    grad_pre = rounded(
        inv_std
        * (
            q_term
            - jnp.mean(q_term, axis=0, keepdims=True)
            - normed * jnp.mean(q_term * normed, axis=0, keepdims=True)
        )
    )
    grad_rim = extended(grad_pre, (("space", 1),), RADIUS)
    grad_padded = jnp.pad(grad_rim, ((0, 0), (0, 0), (RADIUS, RADIUS)))
    back_conv = depthwise(grad_padded, dw_kernel[:, ::-1], strip_w, strip_h)
    grad_image = (pix_f * (cot_f + back_conv)).astype(jnp.bfloat16)
    grad_k = kernel_sums(padded, grad_pre, strip_w, strip_h) * gscale
    vectors = (
        jnp.stack(
            [
                jnp.sum(grad_pre.astype(flt), axis=(1, 2)),
                jnp.sum(grad_ln.astype(flt) * normed, axis=(1, 2)),
                jnp.sum(grad_ln.astype(flt), axis=(1, 2)),
                gb_out,
                jnp.sum(cot_f * pix_f * mlp_out.astype(flt), axis=(1, 2)),
            ],
            axis=0,
        )
        * gscale
    )
    local_mlp = jnp.stack([gw_in, gw_out], axis=0) * gscale
    grad_mlp, grad_kernel, grad_vectors, grad_b_in = summed_everywhere(
        (local_mlp, grad_k, vectors, gb_in * gscale), ("space", "slide")
    )
    return (out_image[None], grad_image[None], grad_mlp, grad_kernel, grad_vectors, grad_b_in)


def solution(mesh):
    placed = (
        P("slide", None, "space", None),
        P("slide", None, "space", None),
        P("slide", "space", None),
        P(),
        P(),
        P(),
        P(),
        P(),
        P(),
        P(),
        P(),
        P(),
    )
    return jax.shard_map(
        on_device,
        mesh=mesh,
        in_specs=placed,
        out_specs=(
            P("slide", None, "space", None),
            P("slide", None, "space", None),
            P(),
            P(),
            P(),
            P(),
        ),
        check_vma=False,
    )
```

```python
import math

import jax
import jax.numpy as jnp
from jax import lax
from jax.sharding import PartitionSpec as P

TP = 16
TROWS = 8
TCOL_DEV = 1
MOST = 8


RADIUS = 3
KERNEL_SIDE = 7
EPSILON = 1e-06
GRAD_COEF = 4.0


def extended(block, sides, width):
    for axis, dim in sides:
        count = lax.axis_size(axis)
        forward = [(i, i + 1) for i in range(count - 1)]
        backward = [(target, source) for source, target in forward]
        low = lax.ppermute(
            lax.slice_in_dim(block, block.shape[dim] - width, None, axis=dim), axis, forward
        )
        high = lax.ppermute(lax.slice_in_dim(block, 0, width, axis=dim), axis, backward)
        block = jnp.concatenate([low, block, high], axis=dim)
    return block


def shifted(values, axis, stride, radix, shift):
    pairs = []
    for i in range(lax.axis_size(axis)):
        digit = (i // stride) % radix
        pairs.append((i, i + ((digit + shift) % radix - digit) * stride))
    return lax.ppermute(values, axis, pairs)


def digit_groups(axes):
    groups = []
    for axis in axes:
        stride, size = 1, lax.axis_size(axis)
        while stride < size:
            radix = 4 if size % (stride * 4) == 0 else 2
            groups.append((axis, stride, radix))
            stride *= radix
    return groups


def summed_everywhere(parts, axes, lanes=128, halvings=1):
    flat = jnp.concatenate([p.reshape(-1) for p in parts])
    rows = -(-flat.shape[0] // lanes)
    rows += (-rows) % 128
    block = jnp.pad(flat, (0, rows * lanes - flat.shape[0])).reshape(rows, lanes)
    steps = []
    groups = digit_groups(axes)
    groups = [groups[1], groups[0]] + groups[2:]
    for number, (axis, stride, radix) in enumerate(groups):
        digit = (lax.axis_index(axis) // stride) % radix
        height, rest = divmod(block.shape[0], radix)
        if rest or number >= halvings:
            stack = jnp.zeros((radix,) + block.shape, block.dtype)
            stack = lax.dynamic_update_index_in_dim(stack, block, digit, 0)
            for shift in range(1, radix):
                got = shifted(block, axis, stride, radix, shift)
                stack = lax.dynamic_update_index_in_dim(stack, got, (digit - shift) % radix, 0)
            block = stack[0]
            for k in range(1, radix):
                block = block + stack[k]
            continue
        keep = lax.dynamic_slice_in_dim(block, digit * height, height)
        for shift in range(1, radix):
            send = lax.dynamic_slice_in_dim(block, ((digit + shift) % radix) * height, height)
            keep = keep + shifted(send, axis, stride, radix, shift)
        block = keep
        steps.append((axis, stride, radix, digit))
    for axis, stride, radix, digit in reversed(steps):
        height = block.shape[0]
        whole = jnp.zeros((height * radix,) + block.shape[1:], block.dtype)
        whole = lax.dynamic_update_slice_in_dim(whole, block, digit * height, 0)
        for shift in range(1, radix):
            got = shifted(block, axis, stride, radix, shift)
            whole = lax.dynamic_update_slice_in_dim(
                whole, got, ((digit - shift) % radix) * height, 0
            )
        block = whole
    flat = block.reshape(-1)
    out, start = [], 0
    for p in parts:
        out.append(flat[start : start + p.size].reshape(p.shape))
        start += p.size
    return tuple(out)

def rounded(values):
    return lax.optimization_barrier(values.astype(jnp.bfloat16))


def gelu_value(values):
    return 0.5 * values * (1.0 + jax.scipy.special.erf(values * (1.0 / math.sqrt(2.0))))


def gelu_slope(values):
    return 0.5 * (1.0 + jax.scipy.special.erf(values * (1.0 / math.sqrt(2.0)))) + values * jnp.exp(
        -0.5 * values * values
    ) * (1.0 / math.sqrt(2.0 * math.pi))


def depthwise(padded, kernel, strip_w, strip_h):
    result = jnp.zeros((padded.shape[0], strip_w, strip_h), jnp.float32)
    for k_row in range(KERNEL_SIDE):
        for k_col in range(KERNEL_SIDE):
            weight = kernel[:, k_row * KERNEL_SIDE + k_col][:, None, None]
            result = result + weight * padded[
                :, k_row : k_row + strip_w, k_col : k_col + strip_h
            ].astype(jnp.float32)
    return result


def kernel_sums(padded, grad_pre, strip_w, strip_h):
    grad_f = grad_pre.astype(jnp.float32)
    entries = []
    for k_row in range(KERNEL_SIDE):
        for k_col in range(KERNEL_SIDE):
            piece = padded[:, k_row : k_row + strip_w, k_col : k_col + strip_h].astype(jnp.float32)
            entries.append(jnp.sum(grad_f * piece, axis=(1, 2)))
    return jnp.stack(entries, axis=1)


def to_tiles(planes):
    channels = planes.shape[0]
    shaped = planes.reshape(channels, TCOL_DEV, TP, TROWS, TP).transpose(1, 3, 0, 2, 4)
    return shaped.reshape(TCOL_DEV * TROWS, channels, TP * TP)


def from_tiles(tiles_in):
    channels = tiles_in.shape[1]
    shaped = tiles_in.reshape(TCOL_DEV, TROWS, channels, TP, TP).transpose(2, 0, 3, 1, 4)
    return shaped.reshape(channels, TCOL_DEV * TP, TROWS * TP)


def mlp_pixels(w_in, w_out, b_in, b_out, x_pix, d_pix):
    flt = jnp.float32
    pre_act = jnp.einsum("cf,cp->fp", w_in, x_pix, preferred_element_type=flt) + b_in[:, None]
    hidden = rounded(gelu_value(pre_act))
    mlp_out = rounded(
        jnp.einsum("cf,fp->cp", w_out, hidden, preferred_element_type=flt) + b_out[:, None]
    )
    back_hid = jnp.einsum("cf,cp->fp", w_out, d_pix, preferred_element_type=flt)
    grad_act = rounded(back_hid * gelu_slope(pre_act))
    grad_ln = rounded(jnp.einsum("cf,fp->cp", w_in, grad_act, preferred_element_type=flt))
    gw_in = jnp.einsum("cp,fp->cf", x_pix, grad_act, preferred_element_type=flt)
    gw_out = jnp.einsum("cp,fp->cf", d_pix, hidden, preferred_element_type=flt)
    gb_in = jnp.sum(grad_act.astype(flt), axis=1)
    gb_out = jnp.sum(d_pix.astype(flt), axis=1)
    return (mlp_out, grad_ln, gw_in, gw_out, gb_in, gb_out)


def on_device(
    image,
    cotangent,
    tissue,
    dw_kernel,
    dw_bias,
    ln_gain,
    ln_bias,
    w_in,
    b_in,
    w_out,
    b_out,
    layer_scale,
):
    flt = jnp.float32
    strip_w = image.shape[2]
    strip_h = image.shape[3]
    gscale = GRAD_COEF / math.sqrt(
        lax.axis_size("space") * lax.axis_size("slide") * strip_w * strip_h
    )
    live_tiles = tissue[0]
    pixel_mask = jnp.repeat(jnp.repeat(live_tiles, TP, axis=0), TP, axis=1).astype(jnp.bfloat16)
    pix_f = pixel_mask[None].astype(flt)
    masked = image[0] * pixel_mask[None]
    rimmed = extended(masked, (("space", 1),), RADIUS)
    padded = jnp.pad(rimmed, ((0, 0), (0, 0), (RADIUS, RADIUS)))
    pre = depthwise(padded, dw_kernel, strip_w, strip_h) + dw_bias[:, None, None]
    centered = pre - jnp.mean(pre, axis=0, keepdims=True)
    inv_std = lax.rsqrt(jnp.mean(centered * centered, axis=0, keepdims=True) + EPSILON)
    normed = centered * inv_std
    ln_out = rounded(normed * ln_gain[:, None, None] + ln_bias[:, None, None])
    cot_f = cotangent[0].astype(flt)
    grad_mix = rounded(cot_f * pix_f * layer_scale[:, None, None])
    channels, pixels = ln_out.shape[0], strip_w * strip_h
    mo_flat, dxh_flat, gw_in, gw_out, gb_in, gb_out = mlp_pixels(
        w_in, w_out, b_in, b_out, ln_out.reshape(channels, pixels), grad_mix.reshape(channels, pixels)
    )
    mlp_out = mo_flat.reshape(ln_out.shape) * pixel_mask[None]
    grad_ln = dxh_flat.reshape(ln_out.shape) * pixel_mask[None]
    out_image = (
        pix_f * (masked.astype(flt) + layer_scale[:, None, None] * mlp_out.astype(flt))
    ).astype(jnp.bfloat16)
    q_term = grad_ln.astype(flt) * ln_gain[:, None, None]
    grad_pre = rounded(
        inv_std
        * (
            q_term
            - jnp.mean(q_term, axis=0, keepdims=True)
            - normed * jnp.mean(q_term * normed, axis=0, keepdims=True)
        )
    )
    grad_rim = extended(grad_pre, (("space", 1),), RADIUS)
    grad_padded = jnp.pad(grad_rim, ((0, 0), (0, 0), (RADIUS, RADIUS)))
    back_conv = depthwise(grad_padded, dw_kernel[:, ::-1], strip_w, strip_h)
    grad_image = (pix_f * (cot_f + back_conv)).astype(jnp.bfloat16)
    grad_k = kernel_sums(padded, grad_pre, strip_w, strip_h) * gscale
    vectors = (
        jnp.stack(
            [
                jnp.sum(grad_pre.astype(flt), axis=(1, 2)),
                jnp.sum(grad_ln.astype(flt) * normed, axis=(1, 2)),
                jnp.sum(grad_ln.astype(flt), axis=(1, 2)),
                gb_out,
                jnp.sum(cot_f * pix_f * mlp_out.astype(flt), axis=(1, 2)),
            ],
            axis=0,
        )
        * gscale
    )
    local_mlp = jnp.stack([gw_in, gw_out], axis=0) * gscale
    grad_mlp, grad_kernel, grad_vectors, grad_b_in = summed_everywhere(
        (local_mlp, grad_k, vectors, gb_in * gscale), ("space", "slide")
    )
    return (out_image[None], grad_image[None], grad_mlp, grad_kernel, grad_vectors, grad_b_in)


def solution(mesh):
    placed = (
        P("slide", None, "space", None),
        P("slide", None, "space", None),
        P("slide", "space", None),
        P(),
        P(),
        P(),
        P(),
        P(),
        P(),
        P(),
        P(),
        P(),
    )
    return jax.shard_map(
        on_device,
        mesh=mesh,
        in_specs=placed,
        out_specs=(
            P("slide", None, "space", None),
            P("slide", None, "space", None),
            P(),
            P(),
            P(),
            P(),
        ),
        check_vma=False,
    )
```

```python
import math

import jax
import jax.numpy as jnp
from jax import lax
from jax.sharding import PartitionSpec as P

TP = 16
TROWS = 8
TCOL_DEV = 1
MOST = 8


RADIUS = 3
KERNEL_SIDE = 7
EPSILON = 1e-06
GRAD_COEF = 4.0


def extended(block, sides, width):
    for axis, dim in sides:
        count = lax.axis_size(axis)
        forward = [(i, i + 1) for i in range(count - 1)]
        backward = [(target, source) for source, target in forward]
        low = lax.ppermute(
            lax.slice_in_dim(block, block.shape[dim] - width, None, axis=dim), axis, forward
        )
        high = lax.ppermute(lax.slice_in_dim(block, 0, width, axis=dim), axis, backward)
        block = jnp.concatenate([low, block, high], axis=dim)
    return block


def shifted(values, axis, stride, radix, shift):
    pairs = []
    for i in range(lax.axis_size(axis)):
        digit = (i // stride) % radix
        pairs.append((i, i + ((digit + shift) % radix - digit) * stride))
    return lax.ppermute(values, axis, pairs)


def digit_groups(axes):
    groups = []
    for axis in axes:
        stride, size = 1, lax.axis_size(axis)
        while stride < size:
            radix = 4 if size % (stride * 4) == 0 else 2
            groups.append((axis, stride, radix))
            stride *= radix
    return groups


def summed_everywhere(parts, axes, lanes=128, halvings=1):
    flat = jnp.concatenate([p.reshape(-1) for p in parts])
    rows = -(-flat.shape[0] // lanes)
    rows += (-rows) % 4
    block = jnp.pad(flat, (0, rows * lanes - flat.shape[0])).reshape(rows, lanes)
    steps = []
    for number, (axis, stride, radix) in enumerate(digit_groups(axes)):
        digit = (lax.axis_index(axis) // stride) % radix
        height, rest = divmod(block.shape[0], radix)
        if rest or number >= halvings:
            stack = jnp.zeros((radix,) + block.shape, block.dtype)
            stack = lax.dynamic_update_index_in_dim(stack, block, digit, 0)
            for shift in range(1, radix):
                got = shifted(block, axis, stride, radix, shift)
                stack = lax.dynamic_update_index_in_dim(stack, got, (digit - shift) % radix, 0)
            block = stack[0]
            for k in range(1, radix):
                block = block + stack[k]
            continue
        keep = lax.dynamic_slice_in_dim(block, digit * height, height)
        for shift in range(1, radix):
            send = lax.dynamic_slice_in_dim(block, ((digit + shift) % radix) * height, height)
            keep = keep + shifted(send, axis, stride, radix, shift)
        block = keep
        steps.append((axis, stride, radix, digit))
    for axis, stride, radix, digit in reversed(steps):
        height = block.shape[0]
        whole = jnp.zeros((height * radix,) + block.shape[1:], block.dtype)
        whole = lax.dynamic_update_slice_in_dim(whole, block, digit * height, 0)
        for shift in range(1, radix):
            got = shifted(block, axis, stride, radix, shift)
            whole = lax.dynamic_update_slice_in_dim(
                whole, got, ((digit - shift) % radix) * height, 0
            )
        block = whole
    flat = block.reshape(-1)
    out, start = [], 0
    for p in parts:
        out.append(flat[start : start + p.size].reshape(p.shape))
        start += p.size
    return tuple(out)

def rounded(values):
    return lax.optimization_barrier(values.astype(jnp.bfloat16))


def gelu_value(values):
    return 0.5 * values * (1.0 + jax.scipy.special.erf(values * (1.0 / math.sqrt(2.0))))


def gelu_slope(values):
    return 0.5 * (1.0 + jax.scipy.special.erf(values * (1.0 / math.sqrt(2.0)))) + values * jnp.exp(
        -0.5 * values * values
    ) * (1.0 / math.sqrt(2.0 * math.pi))


def depthwise(padded, kernel, strip_w, strip_h):
    result = jnp.zeros((padded.shape[0], strip_w, strip_h), jnp.float32)
    for k_row in range(KERNEL_SIDE):
        for k_col in range(KERNEL_SIDE):
            weight = kernel[:, k_row * KERNEL_SIDE + k_col][:, None, None]
            result = result + weight * padded[
                :, k_row : k_row + strip_w, k_col : k_col + strip_h
            ].astype(jnp.float32)
    return result


def kernel_sums(padded, grad_pre, strip_w, strip_h):
    grad_f = grad_pre.astype(jnp.float32)
    entries = []
    for k_row in range(KERNEL_SIDE):
        for k_col in range(KERNEL_SIDE):
            piece = padded[:, k_row : k_row + strip_w, k_col : k_col + strip_h].astype(jnp.float32)
            entries.append(jnp.sum(grad_f * piece, axis=(1, 2)))
    return jnp.stack(entries, axis=1)


def to_tiles(planes):
    channels = planes.shape[0]
    shaped = planes.reshape(channels, TCOL_DEV, TP, TROWS, TP).transpose(1, 3, 0, 2, 4)
    return shaped.reshape(TCOL_DEV * TROWS, channels, TP * TP)


def from_tiles(tiles_in):
    channels = tiles_in.shape[1]
    shaped = tiles_in.reshape(TCOL_DEV, TROWS, channels, TP, TP).transpose(2, 0, 3, 1, 4)
    return shaped.reshape(channels, TCOL_DEV * TP, TROWS * TP)


def mlp_pixels(w_in, w_out, b_in, b_out, x_pix, d_pix):
    flt = jnp.float32
    pre_act = jnp.einsum("cf,cp->fp", w_in, x_pix, preferred_element_type=flt) + b_in[:, None]
    hidden = rounded(gelu_value(pre_act))
    mlp_out = rounded(
        jnp.einsum("cf,fp->cp", w_out, hidden, preferred_element_type=flt) + b_out[:, None]
    )
    back_hid = jnp.einsum("cf,cp->fp", w_out, d_pix, preferred_element_type=flt)
    grad_act = rounded(back_hid * gelu_slope(pre_act))
    grad_ln = rounded(jnp.einsum("cf,fp->cp", w_in, grad_act, preferred_element_type=flt))
    gw_in = jnp.einsum("cp,fp->cf", x_pix, grad_act, preferred_element_type=flt)
    gw_out = jnp.einsum("cp,fp->cf", d_pix, hidden, preferred_element_type=flt)
    gb_in = jnp.sum(grad_act.astype(flt), axis=1)
    gb_out = jnp.sum(d_pix.astype(flt), axis=1)
    return (mlp_out, grad_ln, gw_in, gw_out, gb_in, gb_out)


def on_device(
    image,
    cotangent,
    tissue,
    dw_kernel,
    dw_bias,
    ln_gain,
    ln_bias,
    w_in,
    b_in,
    w_out,
    b_out,
    layer_scale,
):
    flt = jnp.float32
    strip_w = image.shape[2]
    strip_h = image.shape[3]
    gscale = GRAD_COEF / math.sqrt(
        lax.axis_size("space") * lax.axis_size("slide") * strip_w * strip_h
    )
    live_tiles = tissue[0]
    pixel_mask = jnp.repeat(jnp.repeat(live_tiles, TP, axis=0), TP, axis=1).astype(jnp.bfloat16)
    pix_f = pixel_mask[None].astype(flt)
    masked = image[0] * pixel_mask[None]
    rimmed = extended(masked, (("space", 1),), RADIUS)
    padded = jnp.pad(rimmed, ((0, 0), (0, 0), (RADIUS, RADIUS)))
    pre = depthwise(padded, dw_kernel, strip_w, strip_h) + dw_bias[:, None, None]
    centered = pre - jnp.mean(pre, axis=0, keepdims=True)
    inv_std = lax.rsqrt(jnp.mean(centered * centered, axis=0, keepdims=True) + EPSILON)
    normed = centered * inv_std
    ln_out = rounded(normed * ln_gain[:, None, None] + ln_bias[:, None, None])
    cot_f = cotangent[0].astype(flt)
    grad_mix = rounded(cot_f * pix_f * layer_scale[:, None, None])
    channels, pixels = ln_out.shape[0], strip_w * strip_h
    mo_flat, dxh_flat, gw_in, gw_out, gb_in, gb_out = mlp_pixels(
        w_in, w_out, b_in, b_out, ln_out.reshape(channels, pixels), grad_mix.reshape(channels, pixels)
    )
    mlp_out = mo_flat.reshape(ln_out.shape) * pixel_mask[None]
    grad_ln = dxh_flat.reshape(ln_out.shape) * pixel_mask[None]
    out_image = (
        pix_f * (masked.astype(flt) + layer_scale[:, None, None] * mlp_out.astype(flt))
    ).astype(jnp.bfloat16)
    q_term = grad_ln.astype(flt) * ln_gain[:, None, None]
    grad_pre = rounded(
        inv_std
        * (
            q_term
            - jnp.mean(q_term, axis=0, keepdims=True)
            - normed * jnp.mean(q_term * normed, axis=0, keepdims=True)
        )
    )
    grad_rim = extended(grad_pre, (("space", 1),), RADIUS)
    grad_padded = jnp.pad(grad_rim, ((0, 0), (0, 0), (RADIUS, RADIUS)))
    back_conv = depthwise(grad_padded, dw_kernel[:, ::-1], strip_w, strip_h)
    grad_image = (pix_f * (cot_f + back_conv)).astype(jnp.bfloat16)
    grad_k = kernel_sums(padded, grad_pre, strip_w, strip_h) * gscale
    vectors = (
        jnp.stack(
            [
                jnp.sum(grad_pre.astype(flt), axis=(1, 2)),
                jnp.sum(grad_ln.astype(flt) * normed, axis=(1, 2)),
                jnp.sum(grad_ln.astype(flt), axis=(1, 2)),
                gb_out,
                jnp.sum(cot_f * pix_f * mlp_out.astype(flt), axis=(1, 2)),
            ],
            axis=0,
        )
        * gscale
    )
    local_mlp = jnp.stack([gw_in, gw_out], axis=0) * gscale
    grad_mlp, grad_kernel, grad_vectors, grad_b_in = summed_everywhere(
        (local_mlp, grad_k, vectors, gb_in * gscale), ("space", "slide")
    )
    return (out_image[None], grad_image[None], grad_mlp, grad_kernel, grad_vectors, grad_b_in)


def solution(mesh):
    placed = (
        P("slide", None, "space", None),
        P("slide", None, "space", None),
        P("slide", "space", None),
        P(),
        P(),
        P(),
        P(),
        P(),
        P(),
        P(),
        P(),
        P(),
    )
    return jax.shard_map(
        on_device,
        mesh=mesh,
        in_specs=placed,
        out_specs=(
            P("slide", None, "space", None),
            P("slide", None, "space", None),
            P(),
            P(),
            P(),
            P(),
        ),
        check_vma=False,
    )
```
